128 devices in a mesh: comp: 2 (over x_hi), py: 8 (over x_lo, y), px: 8 (over z, core).
Axes of the slice: x: 4 (x_hi: 2, x_lo: 2; x = x_hi * 2 + x_lo), y: 4, z: 4, core: 2. Of those that a mesh axis runs over, the one named last changes fastest.
Arguments:
- current_speeds: float32 [2, 128, 256, 256], P(None, 'py', 'px'), may hold values from -1.2 to 1.2
- thermal_anomaly: float32 [128, 256, 256], P('py', 'px'), may hold values from -6 to 6
- solute_amounts: float32 [16, 64, 512, 256], P(None, ('py', 'px')), may hold values from -6 to 6
- delayed_link_source: float32 [2, 2, 64, 512, 256], P('comp', None, ('py', 'px')), may hold values from -6 to 6
- marine_indicator: int32 [128, 256], replicated, may hold values 0 or 1
- floor_layer_index: int32 [128, 256], replicated, may hold values from 1 to 256
- holder_rank: int32 [64, 64], replicated, may hold values from 0 to 63, each once within a row
- biota_exchange_matrix: float32 [16, 16], replicated, may hold values from -1.5 to 1.5
- photic_absorb_share: float32 [16], replicated, may hold values from -4 to 4
- chroma_loading: float32 [16], replicated, may hold values from -3 to 3
Outputs:
- coupling_out: float32 [2, 2, 64, 512, 256], P('comp', None, ('py', 'px'))
The draws below stay inside these ranges and needn't reach their ends.
Inputs may be any that keep to these rules, and one draw needn't show every extreme that they name: `holder_rank`: each row of owner names every tracer owner once.
All inputs are finite; a program needn't handle non-finite values.
Results may differ from the reference program's by a relative error of at most 0.0001.
Values sent between devices are 32-bit elements; how exact they have to be, the bound alone decides.
A program may use at most 128 MiB of HBM per device.

```python
import jax
import jax.numpy as jnp
from jax import lax

NTR = 16
CY = 16
CX = 32
DEPTH_LAYERS = 256
STEPS = 3
GRID_NORTHINGS = 128
GRID_EASTINGS = 256
NP = 64
CP = 512
SC = 8
N_PY = 8
N_PX = 8


def touch_ends(entries, own_key, low, high):
    dims = entries.shape
    place = [jax.random.randint(jax.random.fold_in(own_key, axis), (), 0, dims[axis]) for axis in range(len(dims))]
    entries = entries.at[tuple(place)].set(low)
    longest = dims.index(max(dims))
    place[longest] = (place[longest] + 1) % dims[longest]
    return entries.at[tuple(place)].set(high)


def level_of(own_key, extent, pieces, least, largest):
    factor_of, own = 1.0, jax.random.fold_in(own_key, 6)
    for dim, shards_of in pieces:
        heights = jnp.exp(jax.random.uniform(jax.random.fold_in(own, dim), (shards_of,), jnp.float32, least / len(pieces), largest / len(pieces)))
        factor_of = factor_of * jnp.repeat(heights, extent[dim] // shards_of).reshape([-1 if axis == dim else 1 for axis in range(len(extent))])
    return factor_of


def scatter_about(stream_key, dims, spread, limit, split=(), held_as=jnp.bfloat16):
    array = spread * jax.random.normal(stream_key, dims, jnp.float32)
    if split:
        array = array * level_of(stream_key, dims, split, -0.22, 0.18)
    return jnp.clip(array, -limit, limit).astype(held_as)


def setup_inputs(seed: int = 0) -> dict:
    keys = jax.random.split(jax.random.key(seed), 11)
    return {
        "current_speeds": scatter_about(keys[0], (2, GRID_NORTHINGS, GRID_EASTINGS, DEPTH_LAYERS), 0.2, 1.2, ((1, 8), (2, 8)), jnp.float32),
        "thermal_anomaly": scatter_about(keys[1], (GRID_NORTHINGS, GRID_EASTINGS, DEPTH_LAYERS), 1.0, 6.0, ((0, 8), (1, 8)), jnp.float32),
        "solute_amounts": scatter_about(keys[2], (NTR, NP, CP, DEPTH_LAYERS), 1.0, 6.0, ((1, 64),), jnp.float32),
        "delayed_link_source": scatter_about(keys[3], (2, 2, NP, CP, DEPTH_LAYERS), 1.0, 6.0, ((0, 2), (2, 64)), jnp.float32),
        "marine_indicator": touch_ends((jax.random.randint(keys[4], (GRID_NORTHINGS, GRID_EASTINGS), 0, 5) < 4).astype(jnp.int32), jax.random.fold_in(keys[4], 1), 0, 1),
        "floor_layer_index": touch_ends(jax.random.randint(keys[5], (GRID_NORTHINGS, GRID_EASTINGS), 1, DEPTH_LAYERS + 1), jax.random.fold_in(keys[5], 1), 1, DEPTH_LAYERS).astype(jnp.int32),
        "holder_rank": jax.vmap(lambda own: jax.random.permutation(own, NP))(jax.random.split(keys[6], NP)).reshape((NP, NP)).astype(jnp.int32),
        "biota_exchange_matrix": scatter_about(keys[7], (NTR, NTR), NTR ** -0.5, 1.5, (), jnp.float32),
        "photic_absorb_share": scatter_about(keys[8], (NTR,), 1.0, 4.0, (), jnp.float32),
        "chroma_loading": scatter_about(keys[9], (NTR,), 0.5, 3.0, (), jnp.float32),
    }


advance_marine = 0.1
spreading = 0.1
viscosity = 0.1
damping = 0.05
heat_gain = 0.2
weight_pull_factor = 0.05
coriolis_scale = 1.0
step_tracer = 0.1
heating_speed = 0.06
uptake_rate = 0.01
water_absorb = (0.02, 0.003)
pigment_absorb = (0.03, 0.004)
surface_light = (40.0, 60.0)


def wet_levels(column_depth):
    levels = jnp.arange(DEPTH_LAYERS, dtype=jnp.int32)
    return (levels < column_depth[..., None]).astype(jnp.float32)


def layer_lookup(pattern):
    row_ids = jnp.arange(DEPTH_LAYERS, dtype=jnp.int32)[:, None]
    col_ids = jnp.arange(DEPTH_LAYERS, dtype=jnp.int32)[None, :]
    if pattern == "above":
        return jnp.where(row_ids < col_ids, 1.0, jnp.where(row_ids == col_ids, 0.5, 0.0)).astype(jnp.float32)
    if pattern == "below":
        return jnp.where(row_ids >= col_ids, 1.0, 0.0).astype(jnp.float32)
    return jnp.where(row_ids < col_ids, 1.0, 0.0).astype(jnp.float32)


def profile_product(values, table):
    return jnp.einsum('...j,jk->...k', values, table, precision=lax.Precision.HIGHEST)


def hydro_balance(thermal_grid):
    return weight_pull_factor * profile_product(thermal_grid, layer_lookup("above"))


def second_derivative_sum(values, submerged_flag):
    return (submerged_flag[1] * (values[1] - values[0]) + submerged_flag[2] * (values[2] - values[0])
            + submerged_flag[3] * (values[3] - values[0]) + submerged_flag[4] * (values[4] - values[0]))


def marine_interior(eastward_speed, northward_speed, thermal_grid, hydraulic_head, submerged_flag, soak_factor, rotation_term):
    eastern_boundary = 0.5 * (eastward_speed[0] + eastward_speed[1]) * submerged_flag[0] * submerged_flag[1]
    western_boundary = 0.5 * (eastward_speed[2] + eastward_speed[0]) * submerged_flag[2] * submerged_flag[0]
    northern_boundary = 0.5 * (northward_speed[0] + northward_speed[3]) * submerged_flag[0] * submerged_flag[3]
    southern_boundary = 0.5 * (northward_speed[4] + northward_speed[0]) * submerged_flag[4] * submerged_flag[0]
    carry_along = (eastern_boundary * 0.5 * (thermal_grid[0] + thermal_grid[1]) - western_boundary * 0.5 * (thermal_grid[2] + thermal_grid[0])
              + northern_boundary * 0.5 * (thermal_grid[0] + thermal_grid[3]) - southern_boundary * 0.5 * (thermal_grid[4] + thermal_grid[0]))
    warming_source = heat_gain * (soak_factor[0] + soak_factor[1])
    warmth_following = submerged_flag[0] * (thermal_grid[0] + advance_marine * (spreading * second_derivative_sum(thermal_grid, submerged_flag) - carry_along + warming_source))
    zonal_push = 0.5 * (submerged_flag[1] * (hydraulic_head[1] - hydraulic_head[0]) + submerged_flag[2] * (hydraulic_head[0] - hydraulic_head[2]))
    merid_push = 0.5 * (submerged_flag[3] * (hydraulic_head[3] - hydraulic_head[0]) + submerged_flag[4] * (hydraulic_head[0] - hydraulic_head[4]))
    zonal_next = submerged_flag[0] * (eastward_speed[0] + advance_marine * (rotation_term * northward_speed[0] - zonal_push
                                                            + viscosity * second_derivative_sum(eastward_speed, submerged_flag) - damping * eastward_speed[0]))
    merid_next = submerged_flag[0] * (northward_speed[0] + advance_marine * (-rotation_term * eastward_speed[0] - merid_push
                                                            + viscosity * second_derivative_sum(northward_speed, submerged_flag) - damping * northward_speed[0]))
    divergence = eastern_boundary - western_boundary + northern_boundary - southern_boundary
    upright_passage = -profile_product(divergence, layer_lookup("below"))
    return warmth_following, zonal_next, merid_next, upright_passage


def solute_interior(solute_amount_status, upright_passage, thermal_grid, radiance_grid, submerged_flag, speed_operator, profit_series):
    empty_level = jnp.zeros_like(solute_amount_status[..., :1])
    upper_passage = jnp.concatenate([empty_level, 0.5 * (solute_amount_status[..., 1:] + solute_amount_status[..., :-1]) * upright_passage[..., 1:]], axis=-1)
    lower_passage = jnp.concatenate([upper_passage[..., 1:], empty_level], axis=-1)
    blending = jnp.einsum('ij,j...->i...', speed_operator, solute_amount_status, precision=lax.Precision.HIGHEST)
    nutrient = solute_amount_status[0]
    saturation = nutrient * nutrient / (1.0 + nutrient * nutrient)
    expansion = uptake_rate * radiance_grid * saturation
    profit_profile = profit_series.reshape((-1,) + (1,) * (solute_amount_status.ndim - 1))
    increment = jnp.exp(heating_speed * thermal_grid) * blending + profit_profile * expansion + lower_passage - upper_passage
    return submerged_flag * (solute_amount_status + step_tracer * increment)


def light_profile(solute_amount_status, submerged_flag, weights):
    chlorophyll = jax.nn.softplus(jnp.einsum('f...,f->...', solute_amount_status, weights, precision=lax.Precision.HIGHEST))
    prefix = layer_lookup("prefix")
    absorbed = []
    radiance_grid = jnp.zeros_like(chlorophyll)
    for band_index in range(2):
        attenuation = water_absorb[band_index] + pigment_absorb[band_index] * chlorophyll
        intensity = surface_light[band_index] * jnp.exp(-profile_product(attenuation, prefix))
        absorbed.append(submerged_flag * intensity * (1.0 - jnp.exp(-attenuation)))
        radiance_grid = radiance_grid + intensity * jnp.exp(-0.5 * attenuation)
    return jnp.stack(absorbed), radiance_grid


def adjoining_cells(values):
    east_side = jnp.roll(values, -1, axis=1)
    west_side = jnp.roll(values, 1, axis=1)
    empty_row = jnp.zeros_like(values[:1])
    north_side = jnp.concatenate([values[1:], empty_row], axis=0)
    south_side = jnp.concatenate([empty_row, values[:-1]], axis=0)
    return (values, east_side, west_side, north_side, south_side)


def to_patches(values):
    fields = values.shape[0]
    return values.reshape(fields, N_PY, CY, N_PX, CX, DEPTH_LAYERS).transpose(0, 1, 3, 2, 4, 5).reshape(fields, NP, CP, DEPTH_LAYERS)


def from_patches(values):
    fields = values.shape[0]
    return values.reshape(fields, N_PY, N_PX, CY, CX, DEPTH_LAYERS).transpose(0, 1, 3, 2, 4, 5).reshape(fields, GRID_NORTHINGS, GRID_EASTINGS, DEPTH_LAYERS)


def owner_inverse(holder_rank):
    indices = jnp.arange(NP, dtype=jnp.int32)
    matches = holder_rank[:, :, None] == indices[None, None, :]
    return jnp.sum(jnp.where(matches, indices[None, :, None], 0), axis=1).astype(jnp.int32)


def to_tracer(patched, inverse):
    fields = patched.shape[0]
    blocks = patched.reshape(fields, NP, NP, SC, DEPTH_LAYERS)
    index_full = jnp.broadcast_to(inverse[None, :, :, None, None], blocks.shape)
    picked = jnp.take_along_axis(blocks, index_full, axis=2)
    return picked.transpose(0, 2, 1, 3, 4).reshape(fields, NP, CP, DEPTH_LAYERS)


def from_tracer(tracer_form, holder_rank):
    fields = tracer_form.shape[0]
    blocks = tracer_form.reshape(fields, NP, NP, SC, DEPTH_LAYERS).transpose(0, 2, 1, 3, 4)
    index_full = jnp.broadcast_to(holder_rank[None, :, :, None, None], blocks.shape)
    picked = jnp.take_along_axis(blocks, index_full, axis=2)
    return picked.reshape(fields, NP, CP, DEPTH_LAYERS)


def reference(current_speeds, thermal_anomaly, solute_amounts, delayed_link_source, marine_indicator, floor_layer_index, holder_rank, biota_exchange_matrix, photic_absorb_share, chroma_loading):
    wet_flow = wet_levels(marine_indicator * floor_layer_index)
    submerged_flag = adjoining_cells(wet_flow)
    inverse = owner_inverse(holder_rank)
    wet_tracer = to_tracer(to_patches(wet_flow[None]), inverse)[0]
    row_ids = jnp.arange(GRID_NORTHINGS, dtype=jnp.int32).astype(jnp.float32)
    rotation_term = (coriolis_scale * (2.0 * (row_ids + 0.5) / GRID_NORTHINGS - 1.0)).reshape(GRID_NORTHINGS, 1, 1)
    eastward_speed = current_speeds[0]
    northward_speed = current_speeds[1]
    thermal_grid = thermal_anomaly
    soak_factor = from_patches(delayed_link_source[0])
    fluxes = delayed_link_source[1]
    solute_amount_status = solute_amounts
    radiance_grid = light_profile(solute_amounts, wet_tracer, chroma_loading)[1]
    for lagged in range(STEPS):
        hydraulic_head = hydro_balance(thermal_grid)
        warmth_following, zonal_next, merid_next, upright_passage = marine_interior(
            adjoining_cells(eastward_speed), adjoining_cells(northward_speed), adjoining_cells(thermal_grid), adjoining_cells(hydraulic_head),
            submerged_flag, soak_factor, rotation_term)
        solute_amount_status = solute_interior(solute_amount_status, fluxes[0], fluxes[1], radiance_grid, wet_tracer, biota_exchange_matrix, photic_absorb_share)
        absorbed, radiance_grid = light_profile(solute_amount_status, wet_tracer, chroma_loading)
        soak_factor = from_patches(from_tracer(absorbed, holder_rank))
        fluxes = to_tracer(to_patches(jnp.stack([upright_passage, warmth_following])), inverse)
        eastward_speed = zonal_next
        northward_speed = merid_next
        thermal_grid = warmth_following
    return jnp.stack([to_patches(soak_factor), fluxes])
```

```python
import jax
import jax.numpy as jnp
from jax import lax
from jax.experimental import pallas as pl
from jax.experimental.pallas import tpu as pltpu
from jax.sharding import PartitionSpec as P

NTR = 16
CY = 16
CX = 32
K = 256
NP = 64
SC = 8
NS = 32
F32 = jnp.float32
BF16 = jnp.bfloat16
MESH = pl.DeviceIdType.MESH


def split(x):
    hi = x.astype(BF16)
    lo = (x - hi.astype(F32)).astype(BF16)
    return hi, lo


def dot(a, b):
    return jnp.dot(a, b, preferred_element_type=F32)


def dot_two(x, table):
    hi, lo = split(x)
    return dot(hi, table) + dot(lo, table)


def kernel(
    inv_s,
    own_s,
    share_s,
    load_s,
    speeds,
    thermal,
    solute,
    link,
    depth_o,
    depth_t,
    mix,
    out,
    b0,
    b1,
    b2,
    press,
    wet_o,
    tabs,
    wmix,
    conc,
    chl_b,
    irr,
    tfl,
    div,
    rise,
    bands0,
    asum0,
    f0r,
    f1s,
    f1r,
    f2s,
    f2r,
    f3s,
    f3r,
    own1,
    own2,
    a1r,
    a2r,
    a3s,
    a3r,
    dummy,
    edge_s,
    edge_r,
    lsem,
    hs_sem,
    hr_sem,
    xs_sem,
    xr_sem,
):
    c = lax.axis_index("comp")
    py = lax.axis_index("py")
    px = lax.axis_index("px")
    me = py * 8 + px
    par = lax.rem(c + me, 2)
    half = lax.div(me, 2)

    def dev(cc, rr):
        return (cc, lax.div(rr, 8), lax.rem(rr, 8))

    ld_uv = pltpu.make_async_copy(speeds, b0.at[0:2, 1:17, 8:40, :], lsem.at[0])
    ld_t = pltpu.make_async_copy(thermal, b0.at[2, 1:17, 8:40, :], lsem.at[1])
    ld_c = pltpu.make_async_copy(solute.at[:, :, par], conc, lsem.at[2])
    ld_uv.start()
    ld_t.start()

    @pl.when(c == 0)
    def _():
        pltpu.make_async_copy(link, bands0, lsem.at[3]).start()

    @pl.when(c == 1)
    def _():
        for f in range(2):
            pltpu.make_async_copy(link.at[f, :, par], f0r.at[:, f], lsem.at[4 + f]).start()

    ld_c.start()

    barrier = pltpu.get_barrier_semaphore()
    flat = c * 64 + me

    @pl.loop(1, 128)
    def _(i):
        d = lax.rem(flat + i, 128)
        pl.semaphore_signal(
            barrier,
            inc=1,
            device_id=(lax.div(d, 64), lax.rem(lax.div(d, 8), 8), lax.rem(d, 8)),
            device_id_type=MESH,
        )

    rows = lax.broadcasted_iota(jnp.int32, (K, K), 0)
    cols = lax.broadcasted_iota(jnp.int32, (K, K), 1)
    tabs[0] = jnp.where(rows < cols, 1.0, jnp.where(rows == cols, 0.5, 0.0)).astype(BF16)
    tabs[1] = jnp.where(rows >= cols, 1.0, 0.0).astype(BF16)
    tabs[2] = jnp.where(rows < cols, 1.0, 0.0).astype(BF16)
    r16 = lax.broadcasted_iota(jnp.int32, (128, 16), 0)
    c16 = lax.broadcasted_iota(jnp.int32, (128, 16), 1)
    spread = jnp.where(lax.shift_right_logical(r16, 3) == c16, 1.0, 0.0).astype(F32)
    r16t = lax.broadcasted_iota(jnp.int32, (16, 128), 0)
    c16t = lax.broadcasted_iota(jnp.int32, (16, 128), 1)
    spread_t = jnp.where(lax.shift_right_logical(c16t, 3) == r16t, 1.0, 0.0).astype(F32)
    wide = jnp.dot(
        jnp.dot(spread, mix[...], precision=lax.Precision.HIGHEST, preferred_element_type=F32),
        spread_t,
        precision=lax.Precision.HIGHEST,
        preferred_element_type=F32,
    )
    r128 = lax.broadcasted_iota(jnp.int32, (128, 128), 0)
    c128 = lax.broadcasted_iota(jnp.int32, (128, 128), 1)
    same = lax.bitwise_and(r128, 7) == lax.bitwise_and(c128, 7)
    wide = jnp.where(same, wide, 0.0)
    whi, wlo = split(wide)
    wmix[0:128, 0:128] = whi
    wmix[0:128, 128:256] = whi
    wmix[128:256, 0:128] = wlo
    wmix[128:256, 128:256] = jnp.zeros((128, 128), BF16)

    lev48 = lax.broadcasted_iota(jnp.int32, (48, 128), 1)

    @pl.loop(0, 18)
    def _(y):
        d = depth_o[y]
        wet_o[y, :, 0:128] = jnp.where(lev48 < d, 1.0, 0.0).astype(F32)
        wet_o[y, :, 128:256] = jnp.where(lev48 + 128 < d, 1.0, 0.0).astype(F32)

    north = (c, lax.rem(py + 1, 8), px)
    south = (c, lax.rem(py + 7, 8), px)
    east = (c, py, lax.rem(px + 1, 8))
    west = (c, py, lax.rem(px + 7, 8))

    def edge_copies(e, b):
        def rc(src, dst, j, who):
            return pltpu.make_async_remote_copy(
                src_ref=src,
                dst_ref=dst,
                send_sem=hs_sem.at[e, j],
                recv_sem=hr_sem.at[e, j],
                device_id=who,
                device_id_type=MESH,
            )

        return (
            rc(b.at[:, 16, 8:40, :], b.at[:, 0, 8:40, :], 0, north),
            rc(b.at[:, 1, 8:40, :], b.at[:, 17, 8:40, :], 1, south),
            rc(edge_s.at[e, 0], edge_r.at[e, 0], 2, east),
            rc(edge_s.at[e, 1], edge_r.at[e, 1], 3, west),
        )

    def stage_edges(e, b):
        for f in range(3):
            edge_s[e, 0, f] = b[f, 1:17, pl.ds(39, 1), :].reshape(CY, K)
            edge_s[e, 1, f] = b[f, 1:17, pl.ds(8, 1), :].reshape(CY, K)

    def send_edges(e, b):
        for copy in edge_copies(e, b):
            copy.start()

    def take_edges(e, b):
        for copy in edge_copies(e, b):
            copy.wait_recv()
        for f in range(3):
            b[f, 1:17, pl.ds(7, 1), :] = edge_r[e, 0, f].reshape(CY, 1, K)
            b[f, 1:17, pl.ds(40, 1), :] = edge_r[e, 1, f].reshape(CY, 1, K)

    def wait_edge_sends(e, b):
        for copy in edge_copies(e, b):
            copy.wait_send()

    def ocean(b, bo, with_flow):
        if with_flow:

            @pl.loop(0, 18)
            def _(y):
                press[y] = 0.05 * dot_two(b[2, y], tabs[0])

        @pl.loop(0, CY)
        def _(y):
            yy = y + 1
            line = (py * CY + y).astype(F32)
            rot = 2.0 * (line + 0.5) / 128.0 - 1.0
            for xb in range(4):
                x0 = 8 + 8 * xb

                def five(ref):
                    return (
                        ref[yy, pl.ds(x0, 8), :],
                        ref[yy, pl.ds(x0 + 1, 8), :],
                        ref[yy, pl.ds(x0 - 1, 8), :],
                        ref[yy + 1, pl.ds(x0, 8), :],
                        ref[yy - 1, pl.ds(x0, 8), :],
                    )

                w = five(wet_o)
                u = five(b.at[0])
                v = five(b.at[1])
                t = five(b.at[2])

                def lap(x):
                    return (
                        w[1] * (x[1] - x[0])
                        + w[2] * (x[2] - x[0])
                        + w[3] * (x[3] - x[0])
                        + w[4] * (x[4] - x[0])
                    )

                wh = 0.5 * w[0]
                fe = (u[0] + u[1]) * (wh * w[1])
                fw = (u[2] + u[0]) * (wh * w[2])
                fn = (v[0] + v[3]) * (wh * w[3])
                fs = (v[4] + v[0]) * (wh * w[4])
                adv = 0.5 * (
                    fe * (t[0] + t[1])
                    - fw * (t[2] + t[0])
                    + fn * (t[0] + t[3])
                    - fs * (t[4] + t[0])
                )
                tn = w[0] * (t[0] + 0.1 * (0.1 * lap(t) - adv))
                s = y * 4 + xb
                tfl[s] = tn
                div[s] = fe - fw + fn - fs
                if with_flow:
                    p = five(press)
                    gx = 0.5 * (w[1] * (p[1] - p[0]) + w[2] * (p[0] - p[2]))
                    gy = 0.5 * (w[3] * (p[3] - p[0]) + w[4] * (p[0] - p[4]))
                    un = w[0] * (
                        u[0] + 0.1 * (rot * v[0] - gx + 0.1 * lap(u) - 0.05 * u[0])
                    )
                    vn = w[0] * (
                        v[0] + 0.1 * (-rot * u[0] - gy + 0.1 * lap(v) - 0.05 * v[0])
                    )
                    bo[0, yy, pl.ds(x0, 8), :] = un
                    bo[1, yy, pl.ds(x0, 8), :] = vn
                    bo[2, yy, pl.ds(x0, 8), :] = tn

        @pl.loop(0, 4)
        def _(i):
            d = div[pl.ds(i * 16, 16)].reshape(128, K)
            rise[pl.ds(i * 16, 16)] = -dot_two(d, tabs[1]).reshape(16, 8, K)

    lev8 = lax.broadcasted_iota(jnp.int32, (8, 128), 1)
    lane = lax.broadcasted_iota(jnp.int32, (8, K), 1)

    def wet_of(n):
        d = depth_t[n]
        return jnp.concatenate(
            [
                jnp.where(lev8 < d, 1.0, 0.0).astype(F32),
                jnp.where(lev8 + 128 < d, 1.0, 0.0).astype(F32),
            ],
            axis=1,
        )

    def first_chl():
        @pl.loop(0, NS)
        def _(n):
            total = load_s[0] * conc[0, n]
            for i in range(1, NTR):
                total = total + load_s[i] * conc[i, n]
            chl_b[n] = total

    def tracer(flux, extra):
        @pl.loop(0, NS)
        def _(n):
            up = flux[n, 0]
            heat = flux[n, 1]
            if extra is not None:
                heat = heat + 0.02 * extra[n]
            wet = wet_of(n)
            warm = (0.1 * wet) * jnp.exp(0.06 * heat)
            scaled = (0.05 * wet) * up
            lower = jnp.where(lane == 0, 0.0, scaled)
            upper = jnp.where(lane == K - 1, 0.0, (0.05 * wet) * pltpu.roll(up, K - 1, 1))
            stay = wet + upper - lower
            c0 = conc[0, n]
            sq = c0 * c0
            grow = (0.001 * wet) * irr[n] * (sq / (1.0 + sq))
            x = conc[:, n].reshape(128, K)
            hi, lo = split(x)
            y = dot(wmix[...], jnp.concatenate([hi, lo], axis=0))
            total = None
            for i in range(NTR):
                ci = conc[i, n]
                blend = y[8 * i : 8 * i + 8] + y[128 + 8 * i : 136 + 8 * i]
                new = (
                    stay * ci
                    + warm * blend
                    + upper * pltpu.roll(ci, K - 1, 1)
                    - lower * pltpu.roll(ci, 1, 1)
                    + share_s[i] * grow
                )
                conc[i, n] = new
                part = load_s[i] * new
                total = part if total is None else total + part
            chl_b[n] = total

    lev_f = lax.broadcasted_iota(jnp.int32, (64, K), 1).astype(F32)

    def light(dest):
        @pl.loop(0, 4)
        def _(i):
            sl = pl.ds(i * 8, 8)
            x = chl_b[sl].reshape(64, K)
            chl = jnp.maximum(x, 0.0) + jnp.log1p(jnp.exp(-jnp.abs(x)))
            pre = dot_two(chl, tabs[2])
            i0 = 40.0 * jnp.exp(-(0.02 * lev_f + 0.03 * pre))
            i1 = 60.0 * jnp.exp(-(0.003 * lev_f + 0.004 * pre))
            h0 = jnp.exp(-0.5 * (0.02 + 0.03 * chl))
            h1 = jnp.exp(-0.5 * (0.003 + 0.004 * chl))
            if dest is not a3s:
                irr[sl] = (i0 * h0 + i1 * h1).reshape(8, 8, K)
            if dest is not None:
                wet = jnp.concatenate([wet_of(i * 8 + j) for j in range(8)], axis=0)
                m0 = wet * i0 * (1.0 - h0 * h0)
                m1 = wet * i1 * (1.0 - h1 * h1)
                if dest is a3s:
                    dest[sl, 0] = m0.reshape(8, 8, K)
                    dest[sl, 1] = m1.reshape(8, 8, K)
                else:
                    dest[sl] = (m0 + m1).reshape(8, 8, K)

    def remote(src, dst, x, who):
        return pltpu.make_async_remote_copy(
            src_ref=src,
            dst_ref=dst,
            send_sem=xs_sem.at[x],
            recv_sem=xr_sem.at[x],
            device_id=who,
            device_id_type=MESH,
        )

    def drain(ref, sem):
        pltpu.make_async_copy(ref, ref, sem).wait()

    def local_twice(src, dst, x):
        pltpu.make_async_copy(src, dst, xr_sem.at[x]).start()
        pltpu.make_async_copy(src, dummy.at[x], xs_sem.at[x]).start()

    def send_flux(x, fs, fr):
        @pl.loop(0, NS)
        def _(m):
            s = inv_s[2 * m + par]
            fs[m, 0] = rise[s]
            fs[m, 1] = tfl[s]

        @pl.loop(0, NS)
        def _(i):
            m = lax.rem(half + i, NS)
            r = 2 * m + par

            @pl.when(r != me)
            def _():
                remote(fs.at[m], fr.at[half], x, dev(c, r)).start()

            @pl.when(r == me)
            def _():
                local_twice(fs.at[m], fr.at[half], x)

    ld_uv.wait()
    ld_t.wait()
    stage_edges(0, b0)
    pl.semaphore_wait(barrier, 127)
    send_edges(0, b0)

    @pl.when(c == 0)
    def _():
        pltpu.make_async_copy(link, bands0, lsem.at[3]).wait()

        @pl.loop(0, 8)
        def _(i):
            sl = pl.ds(i * 4, 4)
            asum0[sl] = bands0[0, sl] + bands0[1, sl]

        remote(asum0, asum0, 0, (1, py, px)).start()

    @pl.when(c == 1)
    def _():
        for f in range(2):
            remote(link.at[f, :, 1 - par], f0r.at[:, f], 1 + f, (0, py, px)).start()
        for f in range(2):
            pltpu.make_async_copy(link.at[f, :, par], f0r.at[:, f], lsem.at[4 + f]).wait()

    ld_c.wait()
    first_chl()
    light(None)
    take_edges(0, b0)
    ocean(b0, b1, True)

    @pl.when(c == 1)
    def _():
        remote(asum0, asum0, 0, (1, py, px)).wait_recv()

    @pl.loop(0, CY)
    def _(y):
        for xb in range(4):
            sl = (y + 1, pl.ds(8 + 8 * xb, 8))
            s = y * 4 + xb
            two = lax.div(s, 2)
            new = tfl[s] + 0.02 * wet_o[y + 1, pl.ds(8 + 8 * xb, 8), :] * asum0[two, xb % 2]
            tfl[s] = new
            b1[2, y + 1, pl.ds(8 + 8 * xb, 8), :] = new

    stage_edges(1, b1)
    send_edges(1, b1)
    send_flux(3, f1s, f1r)

    @pl.when(c == 0)
    def _():
        for f in range(2):
            remote(link.at[f, :, 1 - par], f0r.at[:, f], 1 + f, (0, py, px)).wait_recv()

    tracer(f0r, None)
    light(own1)

    @pl.loop(0, NS)
    def _(i):
        n = lax.rem(half + i, NS)
        remote(own1.at[n], a1r.at[me], 5, dev(1, 2 * n + par)).start()

    take_edges(1, b1)
    ocean(b1, b2, True)
    send_flux(4, f2s, f2r)

    drain(f1r, xr_sem.at[3])
    tracer(f1r, None)
    light(own2)

    @pl.when(c == 0)
    def _():
        remote(own2, a2r, 6, (1, py, px)).start()

    @pl.when(c == 1)
    def _():
        drain(a1r, xr_sem.at[5])

        @pl.loop(0, CY)
        def _(y):
            for xb in range(4):
                s = y * 4 + xb
                b2[2, y + 1, pl.ds(8 + 8 * xb, 8), :] = tfl[s] + 0.02 * a1r[own_s[s]]

        stage_edges(2, b2)
        send_edges(2, b2)
        take_edges(2, b2)
        ocean(b2, None, False)

        @pl.loop(0, NP)
        def _(r):
            s = inv_s[r]
            f3s[r, 0] = rise[s]
            f3s[r, 1] = tfl[s]

        @pl.loop(0, NP)
        def _(i):
            r = lax.rem(me + i, NP)

            @pl.when(r != me)
            def _():
                remote(f3s.at[r], f3r.at[me], 7, dev(1, r)).start()

            @pl.when(r == me)
            def _():
                local_twice(f3s.at[r], f3r.at[me], 7)

    drain(f2r, xr_sem.at[4])
    tracer(f2r, own1)
    light(a3s)

    @pl.loop(0, NS)
    def _(i):
        n = lax.rem(half + i, NS)
        q = 2 * n + par

        @pl.when((c == 1) | (q != me))
        def _():
            remote(a3s.at[n], a3r.at[me], 8, dev(0, q)).start()

        @pl.when((c == 0) & (q == me))
        def _():
            local_twice(a3s.at[n], a3r.at[me], 8)

    wait_edge_sends(0, b0)
    wait_edge_sends(1, b1)
    drain(f1s, xs_sem.at[3])
    drain(f2s, xs_sem.at[4])
    drain(own1, xs_sem.at[5])

    @pl.when(c == 0)
    def _():
        remote(asum0, asum0, 0, (1, py, px)).wait_send()
        remote(own2, a2r, 6, (1, py, px)).wait_send()
        drain(a3r, xr_sem.at[8])

        @pl.loop(0, NP)
        def _(s):
            r = own_s[s]
            out[0, s] = a3r[r, 0]
            out[1, s] = a3r[r, 1]

    @pl.when(c == 1)
    def _():
        for f in range(2):
            remote(link.at[f, :, 1 - par], f0r.at[:, f], 1 + f, (0, py, px)).wait_send()
        wait_edge_sends(2, b2)
        drain(f3s, xs_sem.at[7])
        remote(own2, a2r, 6, (1, py, px)).wait_recv()
        drain(f3r, xr_sem.at[7])

        @pl.loop(0, NS)
        def _(n):
            mine = 2 * n + par
            other = 2 * n + (1 - par)
            out[0, mine] = f3r[mine, 0]
            out[0, other] = f3r[other, 0]
            out[1, mine] = f3r[mine, 1] + 0.02 * own2[n]
            out[1, other] = f3r[other, 1] + 0.02 * a2r[n]

    drain(a3s, xs_sem.at[8])


def shards(
    current_speeds,
    thermal_anomaly,
    solute_amounts,
    delayed_link_source,
    marine_indicator,
    floor_layer_index,
    holder_rank,
    biota_exchange_matrix,
    photic_absorb_share,
    chroma_loading,
):
    comp = lax.axis_index("comp")
    py = lax.axis_index("py")
    px = lax.axis_index("px")
    me = py * 8 + px
    par = (comp + me) % 2
    depth = marine_indicator * floor_layer_index
    wrapped = jnp.concatenate([depth[:, -8:], depth, depth[:, :8]], axis=1)
    padded = jnp.pad(wrapped, ((1, 1), (0, 0)))
    local = lax.dynamic_slice(padded, (py * CY, px * CX), (CY + 2, CX + 16))
    depth_o = jnp.broadcast_to(local[:, :, None], (CY + 2, CX + 16, 128))
    own_row = lax.dynamic_index_in_dim(holder_rank, me, 0, keepdims=False)
    ids = jnp.arange(NP, dtype=jnp.int32)
    inv_row = jnp.sum(jnp.where(own_row[:, None] == ids[None, :], ids[:, None], 0), axis=0)
    hit = (holder_rank == me).reshape(8, 8, 16, 4)
    blocks = depth.reshape(8, 16, 8, 4, 8)
    strip = jnp.sum(jnp.where(hit.transpose(0, 2, 1, 3)[..., None], blocks, 0), axis=(1, 3))
    mine = lax.dynamic_index_in_dim(strip.reshape(NS, 2, SC), par, 1, keepdims=False)
    depth_t = jnp.broadcast_to(mine[:, :, None], (NS, SC, 128))

    any_spec = pl.BlockSpec(memory_space=pl.ANY)
    vmem = pl.BlockSpec(memory_space=pltpu.VMEM)
    smem = pl.BlockSpec(memory_space=pltpu.SMEM)

    def v(*shape, dtype=F32):
        return pltpu.VMEM(shape, dtype)

    dma = pltpu.SemaphoreType.DMA
    res = pl.pallas_call(
        kernel,
        out_shape=jax.ShapeDtypeStruct((2, NP, SC, K), F32),
        in_specs=[smem] * 4 + [any_spec] * 4 + [vmem] * 3,
        out_specs=vmem,
        scratch_shapes=[
            v(3, 18, 48, K),
            v(3, 18, 48, K),
            v(3, 18, 48, K),
            v(18, 48, K),
            v(18, 48, K),
            v(3, K, K, dtype=BF16),
            v(K, K, dtype=BF16),
            v(NTR, NS, SC, K),
            v(NS, SC, K),
            v(NS, SC, K),
            v(NP, SC, K),
            v(NP, SC, K),
            v(NP, SC, K),
            v(2, NS, 2, SC, K),
            v(NS, 2, SC, K),
            v(NS, 2, SC, K),
            v(NS, 2, SC, K),
            v(NS, 2, SC, K),
            v(NS, 2, SC, K),
            v(NS, 2, SC, K),
            v(NP, 2, SC, K),
            v(NP, 2, SC, K),
            v(NS, SC, K),
            v(NS, SC, K),
            v(NP, SC, K),
            v(NS, SC, K),
            v(NS, 2, SC, K),
            v(NP, 2, SC, K),
            v(9, 2, SC, K),
            v(3, 2, 3, CY, K),
            v(3, 2, 3, CY, K),
            dma((6,)),
            dma((3, 4)),
            dma((3, 4)),
            dma((9,)),
            dma((9,)),
        ],
        compiler_params=pltpu.CompilerParams(
            collective_id=0, has_side_effects=True, vmem_limit_bytes=60 * 1024 * 1024
        ),
    )(
        inv_row.astype(jnp.int32),
        own_row,
        photic_absorb_share,
        chroma_loading,
        current_speeds,
        thermal_anomaly,
        solute_amounts.reshape(NTR, NS, 2, SC, K),
        delayed_link_source.reshape(2, NS, 2, SC, K),
        depth_o,
        depth_t,
        biota_exchange_matrix,
    )
    return res.reshape(1, 2, 1, 512, K)


def solution(mesh):
    placed = (
        P(None, "py", "px", None),
        P("py", "px", None),
        P(None, ("py", "px"), None, None),
        P("comp", None, ("py", "px"), None, None),
        P(),
        P(),
        P(),
        P(),
        P(),
        P(),
    )
    return jax.shard_map(
        shards,
        mesh=mesh,
        in_specs=placed,
        out_specs=P("comp", None, ("py", "px"), None, None),
        check_vma=False,
    )
```

```python
import jax
import jax.numpy as jnp
from jax import lax
from jax.experimental import pallas as pl
from jax.experimental.pallas import tpu as pltpu
from jax.sharding import PartitionSpec as P

NTR = 16
CY = 16
CX = 32
K = 256
NP = 64
SC = 8
NS = 32
F32 = jnp.float32
BF16 = jnp.bfloat16
MESH = pl.DeviceIdType.MESH


def split(x):
    hi = x.astype(BF16)
    lo = (x - hi.astype(F32)).astype(BF16)
    return hi, lo


def dot(a, b):
    return jnp.dot(a, b, preferred_element_type=F32)


def dot_two(x, table):
    hi, lo = split(x)
    return dot(hi, table) + dot(lo, table)


def kernel(
    own_s,
    share_s,
    load_s,
    speeds,
    thermal,
    solute,
    link,
    marine,
    floor,
    owners,
    mix,
    out,
    inv_v,
    inv_s,
    depth,
    depth_t,
    pick,
    face_x,
    face_y,
    south_f,
    mixed_a,
    mixed_b,
    b0,
    b1,
    b2,
    press,
    wet_o,
    tabs,
    wmix,
    conc,
    chl_b,
    irr,
    tfl,
    div,
    rise,
    bands0,
    asum0,
    f0r,
    f1s,
    f1r,
    f2s,
    f2r,
    f3s,
    f3r,
    own1,
    own2,
    a1r,
    a2r,
    a3r,
    dummy,
    edge_s,
    edge_r,
    lsem,
    hs_sem,
    hr_sem,
    xs_sem,
    xr_sem,
):
    c = lax.axis_index("comp")
    py = lax.axis_index("py")
    px = lax.axis_index("px")
    me = py * 8 + px
    par = lax.rem(c + me, 2)
    half = lax.div(me, 2)

    def dev(cc, rr):
        return (cc, lax.div(rr, 8), lax.rem(rr, 8))

    def spot_of(i):
        return jnp.minimum(jnp.maximum(inv_s[0, i], 0), NP - 1)

    ld_uv = pltpu.make_async_copy(speeds, b0.at[0:2, 1:17, 0:32, :], lsem.at[0])
    ld_t = pltpu.make_async_copy(thermal, b0.at[2, 1:17, 0:32, :], lsem.at[1])
    ld_c = pltpu.make_async_copy(solute.at[:, :, par], conc, lsem.at[2])

    def ld_link(f):
        return pltpu.make_async_copy(link.at[f, :, par], f0r.at[:, f], lsem.at[4 + f])

    ld_uv.start()
    ld_t.start()

    @pl.when(c == 0)
    def _():
        pltpu.make_async_copy(link, bands0, lsem.at[3]).start()

    @pl.when(c == 1)
    def _():
        for f in range(2):
            ld_link(f).start()

    ld_c.start()

    barrier = pltpu.get_barrier_semaphore()
    for dc in range(2):
        for db in range(8):

            @pl.loop(1 if dc == 0 and db == 0 else 0, 8)
            def _(a, dc=dc, db=db):
                pl.semaphore_signal(
                    barrier,
                    inc=1,
                    device_id=(lax.rem(c + dc, 2), lax.rem(py + a, 8), lax.rem(px + db, 8)),
                    device_id_type=MESH,
                )

    step64 = lax.broadcasted_iota(jnp.int32, (NP, NP), 1).astype(F32)
    row64 = lax.broadcasted_iota(jnp.int32, (NP, NP), 0)
    held = jnp.where(owners[...] == me, 1.0, 0.0).astype(F32)
    placed = jnp.where(
        jnp.broadcast_to(owners[pl.ds(me, 1), :], (NP, NP)) == row64, 1.0, 0.0
    ).astype(F32)
    nt = (((1,), (1,)), ((), ()))
    steps8 = step64[0:8]
    for j, spots in enumerate((placed, held)):
        found = lax.dot_general(steps8, spots, nt, preferred_element_type=F32)
        inv_v[0:8, 64 * j : 64 * j + 64] = jnp.minimum(found, NP - 1.0).astype(jnp.int32)
    to_smem = pltpu.make_async_copy(inv_v, inv_s, lsem.at[6])
    to_smem.start()

    rows = lax.broadcasted_iota(jnp.int32, (K, K), 0)
    cols = lax.broadcasted_iota(jnp.int32, (K, K), 1)
    tabs[0] = jnp.where(rows < cols, 1.0, jnp.where(rows == cols, 0.5, 0.0)).astype(BF16)
    tabs[1] = jnp.where(rows >= cols, 1.0, 0.0).astype(BF16)
    tabs[2] = jnp.where(rows < cols, 1.0, 0.0).astype(BF16)
    r16 = lax.broadcasted_iota(jnp.int32, (128, 16), 0)
    c16 = lax.broadcasted_iota(jnp.int32, (128, 16), 1)
    spread = jnp.where(lax.shift_right_logical(r16, 3) == c16, 1.0, 0.0).astype(F32)
    r16t = lax.broadcasted_iota(jnp.int32, (16, 128), 0)
    c16t = lax.broadcasted_iota(jnp.int32, (16, 128), 1)
    spread_t = jnp.where(lax.shift_right_logical(c16t, 3) == r16t, 1.0, 0.0).astype(F32)
    wide = jnp.dot(
        jnp.dot(spread, mix[...], precision=lax.Precision.HIGHEST, preferred_element_type=F32),
        spread_t,
        precision=lax.Precision.HIGHEST,
        preferred_element_type=F32,
    )
    r128 = lax.broadcasted_iota(jnp.int32, (128, 128), 0)
    c128 = lax.broadcasted_iota(jnp.int32, (128, 128), 1)
    same = lax.bitwise_and(r128, 7) == lax.bitwise_and(c128, 7)
    wide = jnp.where(same, wide, 0.0)
    whi, wlo = split(wide)
    wmix[0:128, 0:128] = whi
    wmix[0:128, 128:256] = whi
    wmix[128:256, 0:128] = wlo
    wmix[128:256, 128:256] = jnp.zeros((128, 128), BF16)

    ones = jnp.ones((K, 128), BF16)
    depth[...] = (marine[...] * floor[...]).astype(F32)
    lev40 = lax.broadcasted_iota(jnp.int32, (40, 128), 1).astype(F32)
    spot = lax.broadcasted_iota(jnp.int32, (40, K), 0)
    spot = jnp.where(spot < 36, spot, spot - 40)
    column = lax.broadcasted_iota(jnp.int32, (40, K), 1)
    chosen = lax.bitwise_and(spot + (px * CX + K), K - 1) == column

    @pl.loop(0, 18)
    def _(y):
        gy = py * CY + y - 1
        inside = jnp.logical_and(gy >= 0, gy < 128)
        line = depth[pl.ds(jnp.clip(gy, 0, 127), 1), :]
        line = line * jnp.where(inside, 1.0, 0.0).astype(F32)
        d = dot(jnp.where(chosen, line, 0.0).astype(BF16), ones)
        w = jnp.concatenate(
            [
                jnp.where(lev40 < d, 1.0, 0.0).astype(F32),
                jnp.where(lev40 + 128.0 < d, 1.0, 0.0).astype(F32),
            ],
            axis=1,
        )
        wet_o[y] = w
        face_x[y] = w * pltpu.roll(w, 39, 0)

    @pl.loop(0, 17)
    def _(y):
        face_y[y] = wet_o[y, 0:32, :] * wet_o[y + 1, 0:32, :]

    to_smem.wait()
    ahead = lax.broadcasted_iota(jnp.int32, (8, K), 1) - lax.broadcasted_iota(
        jnp.int32, (8, K), 0
    )

    @pl.loop(0, NS)
    def _(n):
        q = 2 * n + par
        s = spot_of(64 + q)
        line = depth[lax.div(q, 8) * CY + lax.shift_right_logical(s, 2)]
        x0 = lax.rem(q, 8) * CX + lax.bitwise_and(s, 3) * 8
        pick[n] = jnp.where(ahead == x0, jnp.broadcast_to(line[None, :], (8, K)), 0.0)

    depth_t[...] = dot(pick[...].reshape(NS * 8, K).astype(BF16), ones).reshape(NS, 8, 128)

    north = (c, lax.rem(py + 1, 8), px)
    south = (c, lax.rem(py + 7, 8), px)
    east = (c, py, lax.rem(px + 1, 8))
    west = (c, py, lax.rem(px + 7, 8))

    def edge_copies(e, b, lo, hi):
        def rc(src, dst, j, who):
            return pltpu.make_async_remote_copy(
                src_ref=src,
                dst_ref=dst,
                send_sem=hs_sem.at[e, j],
                recv_sem=hr_sem.at[e, j],
                device_id=who,
                device_id_type=MESH,
            )

        return (
            rc(b.at[lo:hi, 16, 0:32, :], b.at[lo:hi, 0, 0:32, :], 0, north),
            rc(b.at[lo:hi, 1, 0:32, :], b.at[lo:hi, 17, 0:32, :], 1, south),
            rc(edge_s.at[e, 0, lo:hi], edge_r.at[e, 0, lo:hi], 2, east),
            rc(edge_s.at[e, 1, lo:hi], edge_r.at[e, 1, lo:hi], 3, west),
        )

    def send_edges(e, b, lo=0, hi=3):
        for f in range(lo, hi):
            edge_s[e, 0, f] = b[f, 1:17, pl.ds(31, 1), :].reshape(CY, K)
            edge_s[e, 1, f] = b[f, 1:17, pl.ds(0, 1), :].reshape(CY, K)
        if e == 0:
            pl.semaphore_wait(barrier, 127)
        for copy in edge_copies(e, b, lo, hi):
            copy.start()

    def take_edges(e, b, lo=0, hi=3):
        for copy in edge_copies(e, b, lo, hi):
            copy.wait_recv()
        for f in range(lo, hi):
            b[f, 1:17, pl.ds(39, 1), :] = edge_r[e, 0, f].reshape(CY, 1, K)
            b[f, 1:17, pl.ds(32, 1), :] = edge_r[e, 1, f].reshape(CY, 1, K)

    def wait_edge_sends(e, b, lo=0, hi=3):
        for copy in edge_copies(e, b, lo, hi):
            copy.wait_send()

    def ocean(b, bo, flow, heat, passage):
        if flow:

            @pl.loop(0, 6)
            def _(i):
                sl = pl.ds(i * 3, 3)
                t = b[2, sl].reshape(120, K)
                press[sl] = dot_two(t, tabs[0]).reshape(3, 40, K)

        def faces(m, a, t, tn, n, o, on, p, pn):
            through = (0.5 * m) * (a + n)
            m1 = 0.01 * m
            g = first = second = side = None
            if heat:
                g = m1 * (tn - t) - (0.05 * through) * (t + tn)
            if flow:
                spread_a = m1 * (n - a)
                push = (0.05 * 0.05 * m) * (pn - p)
                first = spread_a - push
                second = spread_a + push
                side = m1 * (on - o)
            return through, g, first, second, side

        def face_north(y):
            def pair(ref):
                return ref[y, 0:32, :], ref[y + 1, 0:32, :]

            v, vn = pair(b.at[1])
            t, tn = pair(b.at[2]) if heat else (None, None)
            u, un = pair(b.at[0]) if flow else (None, None)
            p, pn = pair(press) if flow else (None, None)
            return faces(face_y[y], v, t, tn, vn, u, un, p, pn)

        def keep(values):
            for i, value in enumerate(values):
                if value is not None:
                    south_f[i] = value

        keep(face_north(0))

        @pl.loop(0, CY)
        def _(y):
            yy = y + 1

            def pair(ref):
                x = ref[yy]
                return x, pltpu.roll(x, 39, 0)

            def west_of(x):
                return pltpu.roll(x, 1, 0)[0:32]

            u, ue = pair(b.at[0])
            t, te = pair(b.at[2]) if heat else (None, None)
            v, ve = pair(b.at[1]) if flow else (None, None)
            p, pe = pair(press) if flow else (None, None)
            f, g, first, second, side = faces(face_x[yy], u, t, te, ue, v, ve, p, pe)
            north_f = face_north(yy)
            fn, gn, first_n, second_n, side_n = north_f
            s4 = pl.ds(y * 4, 4)
            if passage:
                d = f[0:32] - west_of(f) + fn - south_f[0]
                div[s4] = d.reshape(4, 8, K)
            if heat or flow:
                w = wet_o[yy, 0:32, :]
            if heat:
                new = w * t[0:32] + (g[0:32] - west_of(g)) + (gn - south_f[1])
                tfl[s4] = new.reshape(4, 8, K)
            if flow:
                line = (py * CY + y).astype(F32)
                turn = 0.1 * (2.0 * (line + 0.5) / 128.0 - 1.0)
                wu = w * u[0:32]
                wv = w * v[0:32]
                bo[0, yy, 0:32, :] = (
                    (0.995 * wu + turn * wv)
                    + (first[0:32] - west_of(second))
                    + (side_n - south_f[4])
                )
                bo[1, yy, 0:32, :] = (
                    (0.995 * wv - turn * wu)
                    + (side[0:32] - west_of(side))
                    + (first_n - south_f[3])
                )
            keep(north_f)

        if passage:

            @pl.loop(0, 4)
            def _(i):
                d = div[pl.ds(i * 16, 16)].reshape(128, K)
                rise[pl.ds(i * 16, 16)] = -dot_two(d, tabs[1]).reshape(16, 8, K)

    lev8 = lax.broadcasted_iota(jnp.int32, (8, 128), 1).astype(F32)
    lane = lax.broadcasted_iota(jnp.int32, (8, K), 1)

    def wet_of(n):
        d = depth_t[n]
        return jnp.concatenate(
            [
                jnp.where(lev8 < d, 1.0, 0.0).astype(F32),
                jnp.where(lev8 + 128.0 < d, 1.0, 0.0).astype(F32),
            ],
            axis=1,
        )

    def first_chl():
        @pl.loop(0, NS)
        def _(n):
            total = load_s[0] * conc[0, n]
            for i in range(1, NTR):
                total = total + load_s[i] * conc[i, n]
            chl_b[n] = total

    def mingle(n, dest):
        hi_x, lo_x = split(conc[:, n].reshape(128, K))
        y = dot(wmix[...], jnp.concatenate([hi_x, lo_x], axis=0))
        dest[...] = y[0:128] + y[128:256]

    def tracer(flux, extra, lo, hi):
        def advance(n, mixed):
            up = flux[n, 0]
            heat = flux[n, 1]
            if extra is not None:
                heat = heat + 0.02 * extra[n]
            wet = wet_of(n)
            warm = (0.1 * wet) * jnp.exp(0.06 * heat)
            scaled = (0.05 * wet) * up
            lower = jnp.where(lane == 0, 0.0, scaled)
            upper = jnp.where(lane == K - 1, 0.0, (0.05 * wet) * pltpu.roll(up, K - 1, 1))
            stay = wet + upper - lower
            c0 = conc[0, n]
            sq = c0 * c0
            grow = (0.001 * wet) * irr[n] * (sq / (1.0 + sq))
            total = None
            for i in range(NTR):
                ci = conc[i, n]
                new = (
                    stay * ci
                    + warm * mixed[8 * i : 8 * i + 8]
                    + upper * pltpu.roll(ci, K - 1, 1)
                    - lower * pltpu.roll(ci, 1, 1)
                    + share_s[i] * grow
                )
                conc[i, n] = new
                part = load_s[i] * new
                total = part if total is None else total + part
            chl_b[n] = total

        mingle(lo, mixed_a)

        @pl.loop(0, (hi - lo) // 2)
        def _(k):
            n = lo + 2 * k
            mingle(n + 1, mixed_b)
            advance(n, mixed_a)
            mingle(jnp.minimum(n + 2, hi - 1), mixed_a)
            advance(n + 1, mixed_b)

    lev_f = lax.broadcasted_iota(jnp.int32, (64, K), 1).astype(F32)

    def bands_of(x):
        chl = jnp.maximum(x, 0.0) + jnp.log1p(jnp.exp(-jnp.abs(x)))
        pre = dot_two(chl, tabs[2])
        i0 = 40.0 * jnp.exp(-(0.02 * lev_f + 0.03 * pre))
        i1 = 60.0 * jnp.exp(-(0.003 * lev_f + 0.004 * pre))
        h0 = jnp.exp(-0.5 * (0.02 + 0.03 * chl))
        h1 = jnp.exp(-0.5 * (0.003 + 0.004 * chl))
        return i0, i1, h0, h1

    def light(dest):
        @pl.loop(0, 4)
        def _(i):
            sl = pl.ds(i * 8, 8)
            i0, i1, h0, h1 = bands_of(chl_b[sl].reshape(64, K))
            irr[sl] = (i0 * h0 + i1 * h1).reshape(8, 8, K)
            if dest is not None:
                wet = jnp.concatenate([wet_of(i * 8 + j) for j in range(8)], axis=0)
                total = wet * (i0 * (1.0 - h0 * h0) + i1 * (1.0 - h1 * h1))
                dest[sl] = total.reshape(8, 8, K)

    def remote(src, dst, x, who):
        return pltpu.make_async_remote_copy(
            src_ref=src,
            dst_ref=dst,
            send_sem=xs_sem.at[x],
            recv_sem=xr_sem.at[x],
            device_id=who,
            device_id_type=MESH,
        )

    def drain(ref, sem):
        pltpu.make_async_copy(ref, ref, sem).wait()

    def local_twice(src, dst, x):
        pltpu.make_async_copy(src, dst, xr_sem.at[x]).start()
        pltpu.make_async_copy(src, dummy.at[x], xs_sem.at[x]).start()

    def half_peers(visit):
        for db in range(4):
            bb = lax.rem(lax.div(px, 2) + db, 4)

            @pl.loop(0, 8)
            def _(a, bb=bb):
                row = lax.rem(py + a, 8)
                visit(4 * row + bb, row, 2 * bb + par)

    def start_or_keep(src, dst, x, cc, row, col):
        same = jnp.logical_and(cc == c, jnp.logical_and(row == py, col == px))

        @pl.when(jnp.logical_not(same))
        def _():
            remote(src, dst, x, (cc, row, col)).start()

        @pl.when(same)
        def _():
            local_twice(src, dst, x)

    def send_field(x, f, field, fs, fr):
        @pl.loop(0, 8)
        def _(i):
            for j in range(4):
                m = 4 * i + j
                fs[f, m] = field[spot_of(2 * m + par)]

        def visit(m, row, col):
            start_or_keep(fs.at[f, m], fr.at[half, f], x, c, row, col)

        half_peers(visit)

    def send_all(x, f, field):
        @pl.loop(0, 16)
        def _(i):
            for j in range(4):
                r = 4 * i + j
                f3s[f, r] = field[spot_of(r)]

        for db in range(8):
            col = lax.rem(px + db, 8)

            @pl.loop(0, 8)
            def _(a, col=col):
                row = lax.rem(py + a, 8)
                r = 8 * row + col
                start_or_keep(f3s.at[f, r], f3r.at[f, me], x, 1, row, col)

    def first_heat():
        @pl.loop(0, CY)
        def _(y):
            for xb in range(4):
                s = y * 4 + xb
                two = 2 * y + xb // 2
                new = tfl[s] + 0.02 * wet_o[y + 1, pl.ds(8 * xb, 8), :] * asum0[two, xb % 2]
                tfl[s] = new
                b1[2, y + 1, pl.ds(8 * xb, 8), :] = new

    flux0 = [remote(link.at[f, :, 1 - par], f0r.at[:, f], 1 + f, (0, py, px)) for f in range(2)]
    lagged = remote(asum0, asum0, 0, (1, py, px))
    pair2 = remote(own2, a2r, 8, (1, py, px))

    def second_ocean(c_one):
        ocean(b1, b2, True, True, True)
        if c_one:
            send_edges(2, b2, 0, 2)
        send_field(5, 0, rise, f2s, f2r)
        send_field(6, 1, tfl, f2s, f2r)

    def first_tracer():
        tracer(f0r, None, 0, NS)
        light(own1)

        def visit(n, row, col):
            remote(own1.at[n], a1r.at[me], 7, (1, row, col)).start()

        half_peers(visit)

    ld_uv.wait()
    ld_t.wait()
    send_edges(0, b0)

    @pl.when(c == 0)
    def _():
        pltpu.make_async_copy(link, bands0, lsem.at[3]).wait()

        @pl.loop(0, 8)
        def _(i):
            sl = pl.ds(i * 4, 4)
            asum0[sl] = bands0[0, sl] + bands0[1, sl]

        lagged.start()

    @pl.when(c == 1)
    def _():
        for f in range(2):
            flux0[f].start()
        for f in range(2):
            ld_link(f).wait()

    ld_c.wait()
    first_chl()
    light(None)
    take_edges(0, b0)
    ocean(b0, b1, True, True, True)

    @pl.when(c == 0)
    def _():
        first_heat()
        send_edges(1, b1)
        send_field(3, 0, rise, f1s, f1r)
        send_field(4, 1, tfl, f1s, f1r)
        take_edges(1, b1)
        second_ocean(False)
        for f in range(2):
            flux0[f].wait_recv()
        first_tracer()

    @pl.when(c == 1)
    def _():
        send_edges(1, b1, 0, 2)
        send_field(3, 0, rise, f1s, f1r)
        first_tracer()
        lagged.wait_recv()
        first_heat()
        send_edges(4, b1, 2, 3)
        send_field(4, 1, tfl, f1s, f1r)
        take_edges(1, b1, 0, 2)
        take_edges(4, b1, 2, 3)
        second_ocean(True)

    drain(f1r.at[:, 0], xr_sem.at[3])
    drain(f1r.at[:, 1], xr_sem.at[4])
    tracer(f1r, None, 0, NS)
    light(own2)

    @pl.when(c == 0)
    def _():
        pair2.start()

    @pl.when(c == 1)
    def _():
        take_edges(2, b2, 0, 2)
        ocean(b2, None, False, False, True)
        send_all(9, 0, rise)
        drain(a1r, xr_sem.at[7])

        @pl.loop(0, CY)
        def _(y):
            for xb in range(4):
                s = y * 4 + xb
                b2[2, y + 1, pl.ds(8 * xb, 8), :] = tfl[s] + 0.02 * a1r[own_s[me, s]]

        send_edges(3, b2, 2, 3)

    drain(f2r.at[:, 0], xr_sem.at[5])
    drain(f2r.at[:, 1], xr_sem.at[6])
    for j in range(2):
        tracer(f2r, own1, 16 * j, 16 * j + 16)

        @pl.loop(0, 16)
        def _(k):
            n = 16 * j + k
            start_or_keep(
                chl_b.at[n], a3r.at[me], 11, 0, lax.div(n, 4), 2 * lax.rem(n, 4) + par
            )

        if j == 0:

            @pl.when(c == 1)
            def _():
                take_edges(3, b2, 2, 3)
                ocean(b2, None, False, True, False)
                send_all(10, 1, tfl)

    wait_edge_sends(0, b0)
    drain(f1s.at[0], xs_sem.at[3])
    drain(f1s.at[1], xs_sem.at[4])
    drain(f2s.at[0], xs_sem.at[5])
    drain(f2s.at[1], xs_sem.at[6])
    drain(own1, xs_sem.at[7])

    @pl.when(c == 0)
    def _():
        lagged.wait_send()
        pair2.wait_send()
        wait_edge_sends(1, b1)
        drain(a3r, xr_sem.at[11])

        @pl.loop(0, 8)
        def _(i):
            x = jnp.concatenate([a3r[own_s[me, i * 8 + j]] for j in range(8)], axis=0)
            i0, i1, h0, h1 = bands_of(x)
            wet = jnp.concatenate(
                [
                    wet_o[i * 2 + 1 + j // 4, pl.ds(8 * (j % 4), 8), :]
                    for j in range(8)
                ],
                axis=0,
            )
            sl = pl.ds(i * 8, 8)
            out[0, sl] = (wet * i0 * (1.0 - h0 * h0)).reshape(8, 8, K)
            out[1, sl] = (wet * i1 * (1.0 - h1 * h1)).reshape(8, 8, K)

    @pl.when(c == 1)
    def _():
        for f in range(2):
            flux0[f].wait_send()
        wait_edge_sends(1, b1, 0, 2)
        wait_edge_sends(4, b1, 2, 3)
        wait_edge_sends(2, b2, 0, 2)
        wait_edge_sends(3, b2, 2, 3)
        drain(f3s.at[0], xs_sem.at[9])
        drain(f3s.at[1], xs_sem.at[10])
        pair2.wait_recv()
        drain(f3r.at[0], xr_sem.at[9])
        drain(f3r.at[1], xr_sem.at[10])

        @pl.loop(0, NS)
        def _(n):
            mine = 2 * n + par
            other = 2 * n + (1 - par)
            out[0, mine] = f3r[0, mine]
            out[0, other] = f3r[0, other]
            out[1, mine] = f3r[1, mine] + 0.02 * own2[n]
            out[1, other] = f3r[1, other] + 0.02 * a2r[n]

    drain(chl_b, xs_sem.at[11])


def shards(
    current_speeds,
    thermal_anomaly,
    solute_amounts,
    delayed_link_source,
    marine_indicator,
    floor_layer_index,
    holder_rank,
    biota_exchange_matrix,
    photic_absorb_share,
    chroma_loading,
):
    any_spec = pl.BlockSpec(memory_space=pl.ANY)
    vmem = pl.BlockSpec(memory_space=pltpu.VMEM)
    smem = pl.BlockSpec(memory_space=pltpu.SMEM)

    def v(*shape, dtype=F32):
        return pltpu.VMEM(shape, dtype)

    dma = pltpu.SemaphoreType.DMA
    res = pl.pallas_call(
        kernel,
        out_shape=jax.ShapeDtypeStruct((2, NP, SC, K), F32),
        in_specs=[smem] * 3 + [any_spec] * 4 + [vmem] * 4,
        out_specs=vmem,
        scratch_shapes=[
            v(8, 128, dtype=jnp.int32),
            pltpu.SMEM((8, 128), jnp.int32),
            v(128, K),
            v(NS, SC, 128),
            v(NS, SC, K),
            v(18, 40, K),
            v(17, 32, K),
            v(5, 32, K),
            v(128, K),
            v(128, K),
            v(3, 18, 40, K),
            v(3, 18, 40, K),
            v(3, 18, 40, K),
            v(18, 40, K),
            v(18, 40, K),
            v(3, K, K, dtype=BF16),
            v(K, K, dtype=BF16),
            v(NTR, NS, SC, K),
            v(NS, SC, K),
            v(NS, SC, K),
            v(NP, SC, K),
            v(NP, SC, K),
            v(NP, SC, K),
            v(2, NS, 2, SC, K),
            v(NS, 2, SC, K),
            v(NS, 2, SC, K),
            v(2, NS, SC, K),
            v(NS, 2, SC, K),
            v(2, NS, SC, K),
            v(NS, 2, SC, K),
            v(2, NP, SC, K),
            v(2, NP, SC, K),
            v(NS, SC, K),
            v(NS, SC, K),
            v(NP, SC, K),
            v(NS, SC, K),
            v(NP, SC, K),
            v(12, SC, K),
            v(5, 2, 3, CY, K),
            v(5, 2, 3, CY, K),
            dma((7,)),
            dma((5, 4)),
            dma((5, 4)),
            dma((12,)),
            dma((12,)),
        ],
        compiler_params=pltpu.CompilerParams(
            collective_id=0, has_side_effects=True, vmem_limit_bytes=60 * 1024 * 1024
        ),
    )(
        holder_rank,
        photic_absorb_share,
        chroma_loading,
        current_speeds,
        thermal_anomaly,
        solute_amounts.reshape(NTR, NS, 2, SC, K),
        delayed_link_source.reshape(2, NS, 2, SC, K),
        marine_indicator,
        floor_layer_index,
        holder_rank,
        biota_exchange_matrix,
    )
    return res.reshape(1, 2, 1, 512, K)


def solution(mesh):
    placed = (
        P(None, "py", "px", None),
        P("py", "px", None),
        P(None, ("py", "px"), None, None),
        P("comp", None, ("py", "px"), None, None),
        P(),
        P(),
        P(),
        P(),
        P(),
        P(),
    )
    return jax.shard_map(
        shards,
        mesh=mesh,
        in_specs=placed,
        out_specs=P("comp", None, ("py", "px"), None, None),
        check_vma=False,
    )
```

```python
import jax
import jax.numpy as jnp
from jax import lax
from jax.experimental import pallas as pl
from jax.experimental.pallas import tpu as pltpu
from jax.sharding import PartitionSpec as P

NTR = 16
CY = 16
CX = 32
K = 256
NP = 64
SC = 8
NS = 32
F32 = jnp.float32
BF16 = jnp.bfloat16
MESH = pl.DeviceIdType.MESH


def split(x):
    hi = x.astype(BF16)
    lo = (x - hi.astype(F32)).astype(BF16)
    return hi, lo


def dot(a, b):
    return jnp.dot(a, b, preferred_element_type=F32)


def dot_two(x, table):
    hi, lo = split(x)
    return dot(hi, table) + dot(lo, table)


def kernel(
    own_s,
    share_s,
    load_s,
    speeds,
    thermal,
    solute,
    link,
    marine,
    floor,
    owners,
    mix,
    out,
    inv_v,
    inv_s,
    depth,
    depth_t,
    pick,
    face_x,
    face_y,
    south_f,
    mixed_a,
    mixed_b,
    b0,
    b1,
    b2,
    press,
    wet_o,
    tabs,
    wmix,
    conc,
    chl_b,
    irr,
    tfl,
    div,
    rise,
    bands0,
    asum0,
    f0r,
    f1s,
    f1r,
    f2s,
    f2r,
    f3s,
    f3r,
    own1,
    own2,
    a1r,
    a2r,
    a3r,
    dummy,
    edge_s,
    edge_r,
    lsem,
    hs_sem,
    hr_sem,
    xs_sem,
    xr_sem,
):
    c = lax.axis_index("comp")
    py = lax.axis_index("py")
    px = lax.axis_index("px")
    me = py * 8 + px
    par = lax.rem(c + me, 2)
    half = lax.div(me, 2)

    def dev(cc, rr):
        return (cc, lax.div(rr, 8), lax.rem(rr, 8))

    def spot_of(i):
        return jnp.minimum(jnp.maximum(inv_s[0, i], 0), NP - 1)

    ld_uv = pltpu.make_async_copy(speeds, b0.at[0:2, 1:17, 0:32, :], lsem.at[0])
    ld_t = pltpu.make_async_copy(thermal, b0.at[2, 1:17, 0:32, :], lsem.at[1])
    ld_c = pltpu.make_async_copy(solute.at[:, :, par], conc, lsem.at[2])

    def ld_link(f):
        return pltpu.make_async_copy(link.at[f, :, par], f0r.at[:, f], lsem.at[4 + f])

    ld_uv.start()
    ld_t.start()

    @pl.when(c == 0)
    def _():
        pltpu.make_async_copy(link, bands0, lsem.at[3]).start()

    @pl.when(c == 1)
    def _():
        for f in range(2):
            ld_link(f).start()

    ld_c.start()

    barrier = pltpu.get_barrier_semaphore()
    def greet(dc, a, db):
        pl.semaphore_signal(
            barrier,
            inc=1,
            device_id=(lax.rem(c + dc, 2), lax.rem(py + a, 8), lax.rem(px + db, 8)),
            device_id_type=MESH,
        )

    @pl.loop(1, 8)
    def _(a):
        for db in range(8):
            greet(0, a, db)

    for db in range(1, 8):
        greet(0, 0, db)

    @pl.loop(0, 8)
    def _(a):
        for db in range(8):
            greet(1, a, db)

    north = (c, lax.rem(py + 1, 8), px)
    south = (c, lax.rem(py + 7, 8), px)
    east = (c, py, lax.rem(px + 1, 8))
    west = (c, py, lax.rem(px + 7, 8))

    def edge_copies(e, b, lo, hi):
        def rc(src, dst, j, who):
            return pltpu.make_async_remote_copy(
                src_ref=src,
                dst_ref=dst,
                send_sem=hs_sem.at[e, j],
                recv_sem=hr_sem.at[e, j],
                device_id=who,
                device_id_type=MESH,
            )

        return (
            rc(b.at[lo:hi, 16, 0:32, :], b.at[lo:hi, 0, 0:32, :], 0, north),
            rc(b.at[lo:hi, 1, 0:32, :], b.at[lo:hi, 17, 0:32, :], 1, south),
            rc(edge_s.at[e, 0, lo:hi], edge_r.at[e, 0, lo:hi], 2, east),
            rc(edge_s.at[e, 1, lo:hi], edge_r.at[e, 1, lo:hi], 3, west),
        )

    def send_edges(e, b, lo=0, hi=3):
        for f in range(lo, hi):
            edge_s[e, 0, f] = b[f, 1:17, pl.ds(31, 1), :].reshape(CY, K)
            edge_s[e, 1, f] = b[f, 1:17, pl.ds(0, 1), :].reshape(CY, K)
        if e == 0:
            pl.semaphore_wait(barrier, 127)
        for copy in edge_copies(e, b, lo, hi):
            copy.start()

    def take_edges(e, b, lo=0, hi=3):
        for copy in edge_copies(e, b, lo, hi):
            copy.wait_recv()
        for f in range(lo, hi):
            b[f, 1:17, pl.ds(39, 1), :] = edge_r[e, 0, f].reshape(CY, 1, K)
            b[f, 1:17, pl.ds(32, 1), :] = edge_r[e, 1, f].reshape(CY, 1, K)

    def wait_edge_sends(e, b, lo=0, hi=3):
        for copy in edge_copies(e, b, lo, hi):
            copy.wait_send()

    def ocean(b, bo, flow, heat, passage):
        if flow:

            @pl.loop(0, 6)
            def _(i):
                sl = pl.ds(i * 3, 3)
                t = b[2, sl].reshape(120, K)
                press[sl] = dot_two(t, tabs[0]).reshape(3, 40, K)

        def faces(m, a, t, tn, n, o, on, p, pn):
            through = (0.5 * m) * (a + n)
            m1 = 0.01 * m
            g = first = second = side = None
            if heat:
                g = m1 * (tn - t) - (0.05 * through) * (t + tn)
            if flow:
                spread_a = m1 * (n - a)
                push = (0.05 * 0.05 * m) * (pn - p)
                first = spread_a - push
                second = spread_a + push
                side = m1 * (on - o)
            return through, g, first, second, side

        def face_north(y):
            def pair(ref):
                return ref[y, 0:32, :], ref[y + 1, 0:32, :]

            v, vn = pair(b.at[1])
            t, tn = pair(b.at[2]) if heat else (None, None)
            u, un = pair(b.at[0]) if flow else (None, None)
            p, pn = pair(press) if flow else (None, None)
            return faces(face_y[y], v, t, tn, vn, u, un, p, pn)

        def keep(values):
            for i, value in enumerate(values):
                if value is not None:
                    south_f[i] = value

        keep(face_north(0))

        @pl.loop(0, CY)
        def _(y):
            yy = y + 1

            def pair(ref):
                x = ref[yy]
                return x, pltpu.roll(x, 39, 0)

            def west_of(x):
                return pltpu.roll(x, 1, 0)[0:32]

            u, ue = pair(b.at[0])
            t, te = pair(b.at[2]) if heat else (None, None)
            v, ve = pair(b.at[1]) if flow else (None, None)
            p, pe = pair(press) if flow else (None, None)
            f, g, first, second, side = faces(face_x[yy], u, t, te, ue, v, ve, p, pe)
            north_f = face_north(yy)
            fn, gn, first_n, second_n, side_n = north_f
            s4 = pl.ds(y * 4, 4)
            if passage:
                d = f[0:32] - west_of(f) + fn - south_f[0]
                div[s4] = d.reshape(4, 8, K)
            if heat or flow:
                w = wet_o[yy, 0:32, :]
            if heat:
                new = w * t[0:32] + (g[0:32] - west_of(g)) + (gn - south_f[1])
                tfl[s4] = new.reshape(4, 8, K)
            if flow:
                line = (py * CY + y).astype(F32)
                turn = 0.1 * (2.0 * (line + 0.5) / 128.0 - 1.0)
                wu = w * u[0:32]
                wv = w * v[0:32]
                bo[0, yy, 0:32, :] = (
                    (0.995 * wu + turn * wv)
                    + (first[0:32] - west_of(second))
                    + (side_n - south_f[4])
                )
                bo[1, yy, 0:32, :] = (
                    (0.995 * wv - turn * wu)
                    + (side[0:32] - west_of(side))
                    + (first_n - south_f[3])
                )
            keep(north_f)

        if passage:

            @pl.loop(0, 4)
            def _(i):
                d = div[pl.ds(i * 16, 16)].reshape(128, K)
                rise[pl.ds(i * 16, 16)] = -dot_two(d, tabs[1]).reshape(16, 8, K)

    lev8 = lax.broadcasted_iota(jnp.int32, (8, 128), 1).astype(F32)
    lane = lax.broadcasted_iota(jnp.int32, (8, K), 1)

    def wet_of(n):
        d = depth_t[n]
        return jnp.concatenate(
            [
                jnp.where(lev8 < d, 1.0, 0.0).astype(F32),
                jnp.where(lev8 + 128.0 < d, 1.0, 0.0).astype(F32),
            ],
            axis=1,
        )

    def first_chl():
        @pl.loop(0, NS)
        def _(n):
            total = load_s[0] * conc[0, n]
            for i in range(1, NTR):
                total = total + load_s[i] * conc[i, n]
            chl_b[n] = total

    def mingle(n, dest):
        for j in range(2):
            hi_x, lo_x = split(conc[:, n + j].reshape(128, K))
            y = dot(wmix[...], jnp.concatenate([hi_x, lo_x], axis=0))
            dest[j] = y[0:128] + y[128:256]

    def tracer(flux, extra, lo, hi):
        def advance(n, mixed, j):
            up = flux[n, 0]
            heat = flux[n, 1]
            if extra is not None:
                heat = heat + 0.02 * extra[n]
            wet = wet_of(n)
            warm = (0.1 * wet) * jnp.exp(0.06 * heat)
            scaled = (0.05 * wet) * up
            lower = jnp.where(lane == 0, 0.0, scaled)
            upper = jnp.where(lane == K - 1, 0.0, (0.05 * wet) * pltpu.roll(up, K - 1, 1))
            stay = wet + upper - lower
            c0 = conc[0, n]
            sq = c0 * c0
            grow = (0.001 * wet) * irr[n] * (sq / (1.0 + sq))
            total = None
            for i in range(NTR):
                ci = conc[i, n]
                new = (
                    stay * ci
                    + warm * mixed[j, 8 * i : 8 * i + 8]
                    + upper * pltpu.roll(ci, K - 1, 1)
                    - lower * pltpu.roll(ci, 1, 1)
                    + share_s[i] * grow
                )
                conc[i, n] = new
                part = load_s[i] * new
                total = part if total is None else total + part
            chl_b[n] = total

        mingle(lo, mixed_a)

        @pl.loop(0, (hi - lo) // 4)
        def _(k):
            n = lo + 4 * k
            mingle(n + 2, mixed_b)
            advance(n, mixed_a, 0)
            advance(n + 1, mixed_a, 1)
            mingle(jnp.minimum(n + 4, hi - 2), mixed_a)
            advance(n + 2, mixed_b, 0)
            advance(n + 3, mixed_b, 1)

    lev_f = lax.broadcasted_iota(jnp.int32, (64, K), 1).astype(F32)

    def bands_of(x):
        chl = jnp.maximum(x, 0.0) + jnp.log1p(jnp.exp(-jnp.abs(x)))
        pre = dot_two(chl, tabs[2])
        i0 = 40.0 * jnp.exp(-(0.02 * lev_f + 0.03 * pre))
        i1 = 60.0 * jnp.exp(-(0.003 * lev_f + 0.004 * pre))
        h0 = jnp.exp(-0.5 * (0.02 + 0.03 * chl))
        h1 = jnp.exp(-0.5 * (0.003 + 0.004 * chl))
        return i0, i1, h0, h1

    def light(dest):
        @pl.loop(0, 4)
        def _(i):
            sl = pl.ds(i * 8, 8)
            i0, i1, h0, h1 = bands_of(chl_b[sl].reshape(64, K))
            irr[sl] = (i0 * h0 + i1 * h1).reshape(8, 8, K)
            if dest is not None:
                wet = jnp.concatenate([wet_of(i * 8 + j) for j in range(8)], axis=0)
                total = wet * (i0 * (1.0 - h0 * h0) + i1 * (1.0 - h1 * h1))
                dest[sl] = total.reshape(8, 8, K)

    def remote(src, dst, x, who):
        return pltpu.make_async_remote_copy(
            src_ref=src,
            dst_ref=dst,
            send_sem=xs_sem.at[x],
            recv_sem=xr_sem.at[x],
            device_id=who,
            device_id_type=MESH,
        )

    def drain(ref, sem):
        pltpu.make_async_copy(ref, ref, sem).wait()

    def local_twice(src, dst, x):
        spare = dummy.at[x] if len(src.shape) == 3 else dummy.at[x, 0]
        pltpu.make_async_copy(src, dst, xr_sem.at[x]).start()
        pltpu.make_async_copy(src, spare, xs_sem.at[x]).start()

    strip_cols = [lax.rem(lax.div(px, 2) + db, 4) for db in range(4)]

    def half_peers(visit):
        @pl.loop(1, 8)
        def _(a):
            row = lax.rem(py + a, 8)
            for bb in strip_cols:
                visit(4 * row + bb, row, 2 * bb + par, False)

        for i, bb in enumerate(strip_cols):
            visit(4 * py + bb, py, 2 * bb + par, i == 0)

    def start_or_keep(src, dst, x, cc, row, col):
        same = jnp.logical_and(cc == c, jnp.logical_and(row == py, col == px))

        @pl.when(jnp.logical_not(same))
        def _():
            remote(src, dst, x, (cc, row, col)).start()

        @pl.when(same)
        def _():
            local_twice(src, dst, x)

    def send_field(x, fields, fs, fr, near=False):
        @pl.loop(0, 8)
        def _(i):
            for j in range(4):
                m = 4 * i + j
                s = spot_of(2 * m + par)
                for f, field in fields:
                    fs[m, f] = field[s]

        def visit(m, row, col, maybe):
            if len(fields) == 2:
                src, dst = fs.at[m], fr.at[half]
            else:
                src, dst = fs.at[m, fields[0][0]], fr.at[half, fields[0][0]]
            if maybe:
                start_or_keep(src, dst, x, c, row, col)
            else:
                remote(src, dst, x, (c, row, col)).start()

        if near:

            @pl.loop(0, 4)
            def _(a):
                row = 4 * lax.div(py, 4) + lax.rem(lax.rem(py, 4) + a, 4)
                for bb in strip_cols:
                    visit(4 * row + bb, row, 2 * bb + par, False)

        else:
            half_peers(visit)

    def send_far():
        far = 4 - 4 * lax.div(py, 4)

        @pl.loop(0, 4)
        def _(i):
            for j in range(4):
                s = spot_of(2 * (4 * (far + i) + j) + 1 - par)
                f2s[NS + 4 * i + j, 0] = rise[s]
                f2s[NS + 4 * i + j, 1] = tfl[s]

        @pl.loop(0, 4)
        def _(a):
            i = lax.rem(lax.rem(py, 4) + a, 4)
            for bb in strip_cols:
                who = (1, far + i, 2 * bb + 1 - par)
                remote(f2s.at[NS + 4 * i + bb], f2r.at[half], 5, who).start()

    def send_all(x, f, field, cross):
        @pl.loop(0, 16)
        def _(i):
            for j in range(4):
                r = 4 * i + j
                f3s[f, r] = field[spot_of(r)]

        cols8 = [lax.rem(px + db, 8) for db in range(8)]
        near = 4 * lax.div(py, 4)
        far = 4 - near
        place = lax.rem(py, 4)

        def to_row(row, cols):
            for col in cols:
                remote(f3s.at[f, 8 * row + col], f3r.at[f, me], x, (1, row, col)).start()

        if cross:

            @pl.loop(0, 4)
            def _(a):
                to_row(far + lax.rem(place + a, 4), cols8)

        else:

            @pl.loop(1, 4)
            def _(a):
                to_row(near + lax.rem(place + a, 4), cols8)

            to_row(py, cols8[1:])
            local_twice(f3s.at[f, me], f3r.at[f, me], x)
            if f == 1:

                @pl.loop(0, 4)
                def _(a):
                    to_row(far + lax.rem(place + a, 4), cols8)

    def first_heat():
        @pl.loop(0, CY)
        def _(y):
            s4 = pl.ds(y * 4, 4)
            gain = wet_o[y + 1, 0:32, :] * asum0[pl.ds(2 * y, 2)].reshape(32, K)
            new = tfl[s4].reshape(32, K) + 0.02 * gain
            tfl[s4] = new.reshape(4, 8, K)
            b1[2, y + 1, 0:32, :] = new

    flux0 = [remote(link.at[f, :, 1 - par], f0r.at[:, f], 1 + f, (0, py, px)) for f in range(2)]
    lagged = remote(asum0, asum0, 0, (1, py, px))
    pair2 = remote(own2, a2r, 8, (1, py, px))

    def second_ocean(c_one):
        ocean(b1, b2, True, True, True)
        send_edges(2, b2, 0, 2)
        if c_one:
            send_field(5, [(0, rise), (1, tfl)], f2s, f2r, True)
        else:
            send_field(5, [(0, rise), (1, tfl)], f2s, f2r)
            send_far()

    def first_tracer():
        tracer(f0r, None, 0, NS)
        light(own1)

        def visit(n, row, col, maybe):
            remote(own1.at[n], a1r.at[me], 7, (1, row, col)).start()

        half_peers(visit)

    ld_uv.wait()
    ld_t.wait()
    send_edges(0, b0)

    @pl.when(c == 0)
    def _():
        pltpu.make_async_copy(link, bands0, lsem.at[3]).wait()

        @pl.loop(0, 8)
        def _(i):
            sl = pl.ds(i * 4, 4)
            asum0[sl] = bands0[0, sl] + bands0[1, sl]

        lagged.start()

    @pl.when(c == 1)
    def _():
        for f in range(2):
            flux0[f].start()
        for f in range(2):
            ld_link(f).wait()

    step64 = lax.broadcasted_iota(jnp.int32, (NP, NP), 1).astype(F32)
    row64 = lax.broadcasted_iota(jnp.int32, (NP, NP), 0)
    held = jnp.where(owners[...] == me, 1.0, 0.0).astype(F32)
    placed = jnp.where(
        jnp.broadcast_to(owners[pl.ds(me, 1), :], (NP, NP)) == row64, 1.0, 0.0
    ).astype(F32)
    nt = (((1,), (1,)), ((), ()))
    steps8 = step64[0:8]
    for j, spots in enumerate((placed, held)):
        found = lax.dot_general(steps8, spots, nt, preferred_element_type=F32)
        inv_v[0:8, 64 * j : 64 * j + 64] = jnp.minimum(found, NP - 1.0).astype(jnp.int32)
    to_smem = pltpu.make_async_copy(inv_v, inv_s, lsem.at[6])
    to_smem.start()

    rows = lax.broadcasted_iota(jnp.int32, (K, K), 0)
    cols = lax.broadcasted_iota(jnp.int32, (K, K), 1)
    tabs[0] = jnp.where(rows < cols, 1.0, jnp.where(rows == cols, 0.5, 0.0)).astype(BF16)
    tabs[1] = jnp.where(rows >= cols, 1.0, 0.0).astype(BF16)
    tabs[2] = jnp.where(rows < cols, 1.0, 0.0).astype(BF16)
    r16 = lax.broadcasted_iota(jnp.int32, (128, 16), 0)
    c16 = lax.broadcasted_iota(jnp.int32, (128, 16), 1)
    spread = jnp.where(lax.shift_right_logical(r16, 3) == c16, 1.0, 0.0).astype(F32)
    r16t = lax.broadcasted_iota(jnp.int32, (16, 128), 0)
    c16t = lax.broadcasted_iota(jnp.int32, (16, 128), 1)
    spread_t = jnp.where(lax.shift_right_logical(c16t, 3) == r16t, 1.0, 0.0).astype(F32)
    wide = jnp.dot(
        jnp.dot(spread, mix[...], precision=lax.Precision.HIGHEST, preferred_element_type=F32),
        spread_t,
        precision=lax.Precision.HIGHEST,
        preferred_element_type=F32,
    )
    r128 = lax.broadcasted_iota(jnp.int32, (128, 128), 0)
    c128 = lax.broadcasted_iota(jnp.int32, (128, 128), 1)
    same = lax.bitwise_and(r128, 7) == lax.bitwise_and(c128, 7)
    wide = jnp.where(same, wide, 0.0)
    whi, wlo = split(wide)
    wmix[0:128, 0:128] = whi
    wmix[0:128, 128:256] = whi
    wmix[128:256, 0:128] = wlo
    wmix[128:256, 128:256] = jnp.zeros((128, 128), BF16)

    ones = jnp.ones((K, 128), BF16)
    depth[...] = (marine[...] * floor[...]).astype(F32)
    lev40 = lax.broadcasted_iota(jnp.int32, (40, 128), 1).astype(F32)
    spot = lax.broadcasted_iota(jnp.int32, (40, K), 0)
    spot = jnp.where(spot < 36, spot, spot - 40)
    column = lax.broadcasted_iota(jnp.int32, (40, K), 1)
    chosen = lax.bitwise_and(spot + (px * CX + K), K - 1) == column

    @pl.loop(0, 18)
    def _(y):
        gy = py * CY + y - 1
        inside = jnp.logical_and(gy >= 0, gy < 128)
        line = depth[pl.ds(jnp.clip(gy, 0, 127), 1), :]
        line = line * jnp.where(inside, 1.0, 0.0).astype(F32)
        d = dot(jnp.where(chosen, line, 0.0).astype(BF16), ones)
        w = jnp.concatenate(
            [
                jnp.where(lev40 < d, 1.0, 0.0).astype(F32),
                jnp.where(lev40 + 128.0 < d, 1.0, 0.0).astype(F32),
            ],
            axis=1,
        )
        wet_o[y] = w
        face_x[y] = w * pltpu.roll(w, 39, 0)

    @pl.loop(0, 17)
    def _(y):
        face_y[y] = wet_o[y, 0:32, :] * wet_o[y + 1, 0:32, :]

    to_smem.wait()
    ahead = lax.broadcasted_iota(jnp.int32, (8, K), 1) - lax.broadcasted_iota(
        jnp.int32, (8, K), 0
    )

    @pl.loop(0, 8)
    def _(i):
        for j in range(4):
            n = 4 * i + j
            s = spot_of(64 + 2 * n + par)
            line = depth[i * CY + lax.shift_right_logical(s, 2)]
            x0 = (2 * j + par) * CX + lax.bitwise_and(s, 3) * 8
            pick[n] = jnp.where(ahead == x0, jnp.broadcast_to(line[None, :], (8, K)), 0.0)

    depth_t[...] = dot(pick[...].reshape(NS * 8, K).astype(BF16), ones).reshape(NS, 8, 128)

    ld_c.wait()
    first_chl()
    light(None)
    take_edges(0, b0)
    ocean(b0, b1, True, True, True)

    @pl.when(c == 0)
    def _():
        first_heat()
        send_edges(1, b1)
        send_field(3, [(0, rise), (1, tfl)], f1s, f1r)
        for f in range(2):
            flux0[f].wait_recv()
        first_tracer()
        take_edges(1, b1)
        second_ocean(False)

    @pl.when(c == 1)
    def _():
        send_edges(1, b1, 0, 2)
        send_field(3, [(0, rise)], f1s, f1r)
        first_tracer()
        lagged.wait_recv()
        first_heat()
        send_edges(4, b1, 2, 3)
        send_field(4, [(1, tfl)], f1s, f1r)
        take_edges(1, b1, 0, 2)
        take_edges(4, b1, 2, 3)
        second_ocean(True)

    @pl.when(c == 0)
    def _():
        drain(f1r, xr_sem.at[3])

    @pl.when(c == 1)
    def _():
        drain(f1r.at[:, 0], xr_sem.at[3])
        drain(f1r.at[:, 1], xr_sem.at[4])

    tracer(f1r, None, 0, NS)
    light(own2)

    @pl.when(c == 0)
    def _():
        pair2.start()
        take_edges(2, b2, 0, 2)
        ocean(b2, None, False, False, True)
        send_all(9, 0, rise, True)

    @pl.when(c == 1)
    def _():
        drain(a1r, xr_sem.at[7])

        @pl.loop(0, 8)
        def _(i):
            for j in range(8):
                y = 2 * i + j // 4
                s = 8 * i + j
                b2[2, y + 1, pl.ds(8 * (j % 4), 8), :] = tfl[s] + 0.02 * a1r[own_s[me, s]]

        send_edges(3, b2, 2, 3)
        take_edges(2, b2, 0, 2)
        ocean(b2, None, False, False, True)
        send_all(9, 0, rise, False)

    drain(f2r, xr_sem.at[5])
    for j in range(2):
        tracer(f2r, own1, 16 * j, 16 * j + 16)

        @pl.when(c == 0)
        def _(j=j):
            @pl.loop(0, 16)
            def _(k):
                n = 16 * j + k
                start_or_keep(
                    chl_b.at[n], a3r.at[me], 11, 0, lax.div(n, 4), 2 * lax.rem(n, 4) + par
                )

        @pl.when(c == 1)
        def _(j=j):
            @pl.loop(0, 4)
            def _(a):
                row = 4 * j + lax.rem(py + a, 4)
                for bb in strip_cols:
                    remote(
                        chl_b.at[4 * row + bb], a3r.at[me], 11, (0, row, 2 * bb + par)
                    ).start()

        if j == 0:

            @pl.when(c == 1)
            def _():
                take_edges(3, b2, 2, 3)
                ocean(b2, None, False, True, False)
                send_all(10, 1, tfl, False)

    wait_edge_sends(0, b0)
    drain(own1, xs_sem.at[7])

    @pl.when(c == 0)
    def _():
        lagged.wait_send()
        pair2.wait_send()
        wait_edge_sends(1, b1)
        wait_edge_sends(2, b2, 0, 2)
        drain(f3s.at[0, 0:32], xs_sem.at[9])
        drain(f1s, xs_sem.at[3])
        drain(f2s, xs_sem.at[5])
        drain(a3r, xr_sem.at[11])

        @pl.loop(0, 8)
        def _(i):
            x = jnp.concatenate([a3r[own_s[me, i * 8 + j]] for j in range(8)], axis=0)
            i0, i1, h0, h1 = bands_of(x)
            wet = jnp.concatenate(
                [
                    wet_o[i * 2 + 1 + j // 4, pl.ds(8 * (j % 4), 8), :]
                    for j in range(8)
                ],
                axis=0,
            )
            sl = pl.ds(i * 8, 8)
            out[0, sl] = (wet * i0 * (1.0 - h0 * h0)).reshape(8, 8, K)
            out[1, sl] = (wet * i1 * (1.0 - h1 * h1)).reshape(8, 8, K)

    @pl.when(c == 1)
    def _():
        for f in range(2):
            flux0[f].wait_send()
        drain(f1s.at[:, 0], xs_sem.at[3])
        drain(f2s.at[0:16], xs_sem.at[5])
        drain(f1s.at[:, 1], xs_sem.at[4])
        wait_edge_sends(1, b1, 0, 2)
        wait_edge_sends(4, b1, 2, 3)
        wait_edge_sends(2, b2, 0, 2)
        wait_edge_sends(3, b2, 2, 3)
        drain(f3s.at[0, 0:32], xs_sem.at[9])
        drain(f3s.at[1], xs_sem.at[10])
        pair2.wait_recv()
        drain(f3r.at[0], xr_sem.at[9])
        drain(f3r.at[1], xr_sem.at[10])

        @pl.loop(0, NS)
        def _(n):
            mine = 2 * n + par
            other = 2 * n + (1 - par)
            out[0, mine] = f3r[0, mine]
            out[0, other] = f3r[0, other]
            out[1, mine] = f3r[1, mine] + 0.02 * own2[n]
            out[1, other] = f3r[1, other] + 0.02 * a2r[n]

    drain(chl_b, xs_sem.at[11])


def shards(
    current_speeds,
    thermal_anomaly,
    solute_amounts,
    delayed_link_source,
    marine_indicator,
    floor_layer_index,
    holder_rank,
    biota_exchange_matrix,
    photic_absorb_share,
    chroma_loading,
):
    any_spec = pl.BlockSpec(memory_space=pl.ANY)
    vmem = pl.BlockSpec(memory_space=pltpu.VMEM)
    smem = pl.BlockSpec(memory_space=pltpu.SMEM)

    def v(*shape, dtype=F32):
        return pltpu.VMEM(shape, dtype)

    dma = pltpu.SemaphoreType.DMA
    res = pl.pallas_call(
        kernel,
        out_shape=jax.ShapeDtypeStruct((2, NP, SC, K), F32),
        in_specs=[smem] * 3 + [any_spec] * 4 + [vmem] * 4,
        out_specs=vmem,
        scratch_shapes=[
            v(8, 128, dtype=jnp.int32),
            pltpu.SMEM((8, 128), jnp.int32),
            v(128, K),
            v(NS, SC, 128),
            v(NS, SC, K),
            v(18, 40, K),
            v(17, 32, K),
            v(5, 32, K),
            v(2, 128, K),
            v(2, 128, K),
            v(3, 18, 40, K),
            v(3, 18, 40, K),
            v(3, 18, 40, K),
            v(18, 40, K),
            v(18, 40, K),
            v(3, K, K, dtype=BF16),
            v(K, K, dtype=BF16),
            v(NTR, NS, SC, K),
            v(NS, SC, K),
            v(NS, SC, K),
            v(NP, SC, K),
            v(NP, SC, K),
            v(NP, SC, K),
            v(2, NS, 2, SC, K),
            v(NS, 2, SC, K),
            v(NS, 2, SC, K),
            v(NS, 2, SC, K),
            v(NS, 2, SC, K),
            v(48, 2, SC, K),
            v(NS, 2, SC, K),
            v(2, NP, SC, K),
            v(2, NP, SC, K),
            v(NS, SC, K),
            v(NS, SC, K),
            v(NP, SC, K),
            v(NS, SC, K),
            v(NP, SC, K),
            v(12, 2, SC, K),
            v(5, 2, 3, CY, K),
            v(5, 2, 3, CY, K),
            dma((7,)),
            dma((5, 4)),
            dma((5, 4)),
            dma((12,)),
            dma((12,)),
        ],
        compiler_params=pltpu.CompilerParams(
            collective_id=0, has_side_effects=True, vmem_limit_bytes=60 * 1024 * 1024
        ),
    )(
        holder_rank,
        photic_absorb_share,
        chroma_loading,
        current_speeds,
        thermal_anomaly,
        solute_amounts.reshape(NTR, NS, 2, SC, K),
        delayed_link_source.reshape(2, NS, 2, SC, K),
        marine_indicator,
        floor_layer_index,
        holder_rank,
        biota_exchange_matrix,
    )
    return res.reshape(1, 2, 1, 512, K)


def solution(mesh):
    placed = (
        P(None, "py", "px", None),
        P("py", "px", None),
        P(None, ("py", "px"), None, None),
        P("comp", None, ("py", "px"), None, None),
        P(),
        P(),
        P(),
        P(),
        P(),
        P(),
    )
    return jax.shard_map(
        shards,
        mesh=mesh,
        in_specs=placed,
        out_specs=P("comp", None, ("py", "px"), None, None),
        check_vma=False,
    )
```

```python
import jax
import jax.numpy as jnp
from jax import lax
from jax.experimental import pallas as pl
from jax.experimental.pallas import tpu as pltpu
from jax.sharding import PartitionSpec as P

NTR = 16
CY = 16
CX = 32
K = 256
NP = 64
SC = 8
NS = 32
F32 = jnp.float32
BF16 = jnp.bfloat16
MESH = pl.DeviceIdType.MESH


def split(x):
    hi = x.astype(BF16)
    lo = (x - hi.astype(F32)).astype(BF16)
    return hi, lo


def dot(a, b):
    return jnp.dot(a, b, preferred_element_type=F32)


def dot_two(x, table):
    hi, lo = split(x)
    return dot(hi, table) + dot(lo, table)


def kernel(
    own_s,
    share_s,
    load_s,
    speeds,
    thermal,
    solute,
    link,
    marine,
    floor,
    owners,
    mix,
    out,
    inv_v,
    inv_s,
    depth,
    depth_t,
    pick,
    face_x,
    face_y,
    south_f,
    mixed_a,
    mixed_b,
    b0,
    b1,
    b2,
    press,
    wet_o,
    tabs,
    wmix,
    conc,
    chl_b,
    irr,
    tfl,
    div,
    rise,
    bands0,
    asum0,
    f0r,
    f1s,
    f1r,
    f2s,
    f2r,
    f3s,
    f3r,
    own1,
    own2,
    a1r,
    a2r,
    a3r,
    dummy,
    edge_s,
    edge_r,
    lsem,
    hs_sem,
    hr_sem,
    xs_sem,
    xr_sem,
):
    c = lax.axis_index("comp")
    py = lax.axis_index("py")
    px = lax.axis_index("px")
    me = py * 8 + px
    par = lax.rem(c + me, 2)
    half = lax.div(me, 2)

    def dev(cc, rr):
        return (cc, lax.div(rr, 8), lax.rem(rr, 8))

    def spot_of(i):
        return jnp.minimum(jnp.maximum(inv_s[0, i], 0), NP - 1)

    ld_uv = pltpu.make_async_copy(speeds, b0.at[0:2, 1:17, 0:32, :], lsem.at[0])
    ld_t = pltpu.make_async_copy(thermal, b0.at[2, 1:17, 0:32, :], lsem.at[1])
    ld_c = pltpu.make_async_copy(solute.at[:, :, par], conc, lsem.at[2])

    def ld_link(f):
        return pltpu.make_async_copy(link.at[f, :, par], f0r.at[:, f], lsem.at[4 + f])

    ld_uv.start()
    ld_t.start()

    @pl.when(c == 0)
    def _():
        pltpu.make_async_copy(link, bands0, lsem.at[3]).start()

    @pl.when(c == 1)
    def _():
        for f in range(2):
            ld_link(f).start()

    ld_c.start()

    barrier = pltpu.get_barrier_semaphore()
    def greet(dc, a, db):
        pl.semaphore_signal(
            barrier,
            inc=1,
            device_id=(lax.rem(c + dc, 2), lax.rem(py + a, 8), lax.rem(px + db, 8)),
            device_id_type=MESH,
        )

    @pl.loop(1, 8)
    def _(a):
        for db in range(8):
            greet(0, a, db)

    for db in range(1, 8):
        greet(0, 0, db)

    @pl.loop(0, 8)
    def _(a):
        for db in range(8):
            greet(1, a, db)

    north = (c, lax.rem(py + 1, 8), px)
    south = (c, lax.rem(py + 7, 8), px)
    east = (c, py, lax.rem(px + 1, 8))
    west = (c, py, lax.rem(px + 7, 8))

    def edge_copies(e, b, lo, hi):
        def rc(src, dst, j, who):
            return pltpu.make_async_remote_copy(
                src_ref=src,
                dst_ref=dst,
                send_sem=hs_sem.at[e, j],
                recv_sem=hr_sem.at[e, j],
                device_id=who,
                device_id_type=MESH,
            )

        return (
            rc(b.at[lo:hi, 16, 0:32, :], b.at[lo:hi, 0, 0:32, :], 0, north),
            rc(b.at[lo:hi, 1, 0:32, :], b.at[lo:hi, 17, 0:32, :], 1, south),
            rc(edge_s.at[e, 0, lo:hi], edge_r.at[e, 0, lo:hi], 2, east),
            rc(edge_s.at[e, 1, lo:hi], edge_r.at[e, 1, lo:hi], 3, west),
        )

    def send_edges(e, b, lo=0, hi=3):
        for f in range(lo, hi):
            edge_s[e, 0, f] = b[f, 1:17, pl.ds(31, 1), :].reshape(CY, K)
            edge_s[e, 1, f] = b[f, 1:17, pl.ds(0, 1), :].reshape(CY, K)
        if e == 0:
            pl.semaphore_wait(barrier, 127)
        for copy in edge_copies(e, b, lo, hi):
            copy.start()

    def take_edges(e, b, lo=0, hi=3):
        for copy in edge_copies(e, b, lo, hi):
            copy.wait_recv()
        for f in range(lo, hi):
            b[f, 1:17, pl.ds(39, 1), :] = edge_r[e, 0, f].reshape(CY, 1, K)
            b[f, 1:17, pl.ds(32, 1), :] = edge_r[e, 1, f].reshape(CY, 1, K)

    def wait_edge_sends(e, b, lo=0, hi=3):
        for copy in edge_copies(e, b, lo, hi):
            copy.wait_send()

    def ocean(b, bo, flow, heat, passage):
        if flow:

            @pl.loop(0, 6)
            def _(i):
                sl = pl.ds(i * 3, 3)
                t = b[2, sl].reshape(120, K)
                press[sl] = dot_two(t, tabs[0]).reshape(3, 40, K)

        def faces(m, a, t, tn, n, o, on, p, pn):
            through = (0.5 * m) * (a + n)
            m1 = 0.01 * m
            g = first = second = side = None
            if heat:
                g = m1 * (tn - t) - (0.05 * through) * (t + tn)
            if flow:
                spread_a = m1 * (n - a)
                push = (0.05 * 0.05 * m) * (pn - p)
                first = spread_a - push
                second = spread_a + push
                side = m1 * (on - o)
            return through, g, first, second, side

        def face_north(y):
            def pair(ref):
                return ref[y, 0:32, :], ref[y + 1, 0:32, :]

            v, vn = pair(b.at[1])
            t, tn = pair(b.at[2]) if heat else (None, None)
            u, un = pair(b.at[0]) if flow else (None, None)
            p, pn = pair(press) if flow else (None, None)
            return faces(face_y[y], v, t, tn, vn, u, un, p, pn)

        def keep(values):
            for i, value in enumerate(values):
                if value is not None:
                    south_f[i] = value

        keep(face_north(0))

        @pl.loop(0, CY)
        def _(y):
            yy = y + 1

            def pair(ref):
                x = ref[yy]
                return x, pltpu.roll(x, 39, 0)

            def west_of(x):
                return pltpu.roll(x, 1, 0)[0:32]

            u, ue = pair(b.at[0])
            t, te = pair(b.at[2]) if heat else (None, None)
            v, ve = pair(b.at[1]) if flow else (None, None)
            p, pe = pair(press) if flow else (None, None)
            f, g, first, second, side = faces(face_x[yy], u, t, te, ue, v, ve, p, pe)
            north_f = face_north(yy)
            fn, gn, first_n, second_n, side_n = north_f
            s4 = pl.ds(y * 4, 4)
            if passage:
                d = f[0:32] - west_of(f) + fn - south_f[0]
                div[s4] = d.reshape(4, 8, K)
            if heat or flow:
                w = wet_o[yy, 0:32, :]
            if heat:
                new = w * t[0:32] + (g[0:32] - west_of(g)) + (gn - south_f[1])
                tfl[s4] = new.reshape(4, 8, K)
            if flow:
                line = (py * CY + y).astype(F32)
                turn = 0.1 * (2.0 * (line + 0.5) / 128.0 - 1.0)
                wu = w * u[0:32]
                wv = w * v[0:32]
                bo[0, yy, 0:32, :] = (
                    (0.995 * wu + turn * wv)
                    + (first[0:32] - west_of(second))
                    + (side_n - south_f[4])
                )
                bo[1, yy, 0:32, :] = (
                    (0.995 * wv - turn * wu)
                    + (side[0:32] - west_of(side))
                    + (first_n - south_f[3])
                )
            keep(north_f)

        if passage:

            @pl.loop(0, 4)
            def _(i):
                d = div[pl.ds(i * 16, 16)].reshape(128, K)
                rise[pl.ds(i * 16, 16)] = -dot_two(d, tabs[1]).reshape(16, 8, K)

    lev8 = lax.broadcasted_iota(jnp.int32, (8, 128), 1).astype(F32)
    lane = lax.broadcasted_iota(jnp.int32, (8, K), 1)

    def wet_of(n):
        d = depth_t[n]
        return jnp.concatenate(
            [
                jnp.where(lev8 < d, 1.0, 0.0).astype(F32),
                jnp.where(lev8 + 128.0 < d, 1.0, 0.0).astype(F32),
            ],
            axis=1,
        )

    def first_chl():
        @pl.loop(0, NS)
        def _(n):
            total = load_s[0] * conc[0, n]
            for i in range(1, NTR):
                total = total + load_s[i] * conc[i, n]
            chl_b[n] = total

    def mingle(n, dest):
        for j in range(2):
            hi_x, lo_x = split(conc[:, n + j].reshape(128, K))
            y = dot(wmix[...], jnp.concatenate([hi_x, lo_x], axis=0))
            dest[j] = y[0:128] + y[128:256]

    def tracer(flux, extra, lo, hi):
        def advance(n, mixed, j):
            up = flux[n, 0]
            heat = flux[n, 1]
            if extra is not None:
                heat = heat + 0.02 * extra[n]
            wet = wet_of(n)
            warm = (0.1 * wet) * jnp.exp(0.06 * heat)
            scaled = (0.05 * wet) * up
            lower = jnp.where(lane == 0, 0.0, scaled)
            upper = jnp.where(lane == K - 1, 0.0, (0.05 * wet) * pltpu.roll(up, K - 1, 1))
            stay = wet + upper - lower
            c0 = conc[0, n]
            sq = c0 * c0
            grow = (0.001 * wet) * irr[n] * (sq / (1.0 + sq))
            total = None
            for i in range(NTR):
                ci = conc[i, n]
                new = (
                    stay * ci
                    + warm * mixed[j, 8 * i : 8 * i + 8]
                    + upper * pltpu.roll(ci, K - 1, 1)
                    - lower * pltpu.roll(ci, 1, 1)
                    + share_s[i] * grow
                )
                conc[i, n] = new
                part = load_s[i] * new
                total = part if total is None else total + part
            chl_b[n] = total

        mingle(lo, mixed_a)

        @pl.loop(0, (hi - lo) // 4)
        def _(k):
            n = lo + 4 * k
            mingle(n + 2, mixed_b)
            advance(n, mixed_a, 0)
            advance(n + 1, mixed_a, 1)
            mingle(jnp.minimum(n + 4, hi - 2), mixed_a)
            advance(n + 2, mixed_b, 0)
            advance(n + 3, mixed_b, 1)

    lev_f = lax.broadcasted_iota(jnp.int32, (64, K), 1).astype(F32)

    def bands_of(x):
        chl = jnp.maximum(x, 0.0) + jnp.log1p(jnp.exp(-jnp.abs(x)))
        pre = dot_two(chl, tabs[2])
        i0 = 40.0 * jnp.exp(-(0.02 * lev_f + 0.03 * pre))
        i1 = 60.0 * jnp.exp(-(0.003 * lev_f + 0.004 * pre))
        h0 = jnp.exp(-0.5 * (0.02 + 0.03 * chl))
        h1 = jnp.exp(-0.5 * (0.003 + 0.004 * chl))
        return i0, i1, h0, h1

    def light(dest):
        @pl.loop(0, 4)
        def _(i):
            sl = pl.ds(i * 8, 8)
            i0, i1, h0, h1 = bands_of(chl_b[sl].reshape(64, K))
            irr[sl] = (i0 * h0 + i1 * h1).reshape(8, 8, K)
            if dest is not None:
                wet = jnp.concatenate([wet_of(i * 8 + j) for j in range(8)], axis=0)
                total = wet * (i0 * (1.0 - h0 * h0) + i1 * (1.0 - h1 * h1))
                dest[sl] = total.reshape(8, 8, K)

    def remote(src, dst, x, who):
        return pltpu.make_async_remote_copy(
            src_ref=src,
            dst_ref=dst,
            send_sem=xs_sem.at[x],
            recv_sem=xr_sem.at[x],
            device_id=who,
            device_id_type=MESH,
        )

    def drain(ref, sem):
        pltpu.make_async_copy(ref, ref, sem).wait()

    def local_twice(src, dst, x):
        spare = dummy.at[x] if len(src.shape) == 3 else dummy.at[x, 0]
        pltpu.make_async_copy(src, dst, xr_sem.at[x]).start()
        pltpu.make_async_copy(src, spare, xs_sem.at[x]).start()

    strip_cols = [lax.rem(lax.div(px, 2) + db, 4) for db in range(4)]

    def half_peers(visit):
        @pl.loop(1, 8)
        def _(a):
            row = lax.rem(py + a, 8)
            for bb in strip_cols:
                visit(4 * row + bb, row, 2 * bb + par, False)

        for i, bb in enumerate(strip_cols):
            visit(4 * py + bb, py, 2 * bb + par, i == 0)

    def start_or_keep(src, dst, x, cc, row, col):
        same = jnp.logical_and(cc == c, jnp.logical_and(row == py, col == px))

        @pl.when(jnp.logical_not(same))
        def _():
            remote(src, dst, x, (cc, row, col)).start()

        @pl.when(same)
        def _():
            local_twice(src, dst, x)

    def send_field(x, fields, fs, fr, near=False):
        @pl.loop(0, 8)
        def _(i):
            for j in range(4):
                m = 4 * i + j
                s = spot_of(2 * m + par)
                for f, field in fields:
                    fs[m, f] = field[s]

        def visit(m, row, col, maybe):
            if len(fields) == 2:
                src, dst = fs.at[m], fr.at[half]
            else:
                src, dst = fs.at[m, fields[0][0]], fr.at[half, fields[0][0]]
            if maybe:
                start_or_keep(src, dst, x, c, row, col)
            else:
                remote(src, dst, x, (c, row, col)).start()

        if near:

            @pl.loop(0, 4)
            def _(a):
                row = 4 * lax.div(py, 4) + lax.rem(lax.rem(py, 4) + a, 4)
                for bb in strip_cols:
                    visit(4 * row + bb, row, 2 * bb + par, False)

        else:
            half_peers(visit)

    def send_far():
        far = 4 - 4 * lax.div(py, 4)

        @pl.loop(0, 4)
        def _(i):
            for j in range(4):
                s = spot_of(2 * (4 * (far + i) + j) + 1 - par)
                f2s[NS + 4 * i + j, 0] = rise[s]
                f2s[NS + 4 * i + j, 1] = tfl[s]

        @pl.loop(0, 4)
        def _(a):
            i = lax.rem(lax.rem(py, 4) + a, 4)
            for bb in strip_cols:
                who = (1, far + i, 2 * bb + 1 - par)
                remote(f2s.at[NS + 4 * i + bb], f2r.at[half], 5, who).start()

    def send_all(x, f, field, cross):
        @pl.loop(0, 16)
        def _(i):
            for j in range(4):
                r = 4 * i + j
                f3s[f, r] = field[spot_of(r)]

        cols8 = [lax.rem(px + db, 8) for db in range(8)]
        near = 4 * lax.div(py, 4)
        far = 4 - near
        place = lax.rem(py, 4)

        def to_row(row, cols):
            for col in cols:
                remote(f3s.at[f, 8 * row + col], f3r.at[f, me], x, (1, row, col)).start()

        if cross:

            @pl.loop(0, 4)
            def _(a):
                to_row(far + lax.rem(place + a, 4), cols8)

        else:

            @pl.loop(1, 4)
            def _(a):
                to_row(near + lax.rem(place + a, 4), cols8)

            to_row(py, cols8[1:])
            local_twice(f3s.at[f, me], f3r.at[f, me], x)
            if f == 1:

                @pl.loop(0, 4)
                def _(a):
                    to_row(far + lax.rem(place + a, 4), cols8)

    def first_heat():
        @pl.loop(0, CY)
        def _(y):
            s4 = pl.ds(y * 4, 4)
            gain = wet_o[y + 1, 0:32, :] * asum0[pl.ds(2 * y, 2)].reshape(32, K)
            new = tfl[s4].reshape(32, K) + 0.02 * gain
            tfl[s4] = new.reshape(4, 8, K)
            b1[2, y + 1, 0:32, :] = new

    flux0 = [remote(link.at[f, :, 1 - par], f0r.at[:, f], 1 + f, (0, py, px)) for f in range(2)]
    lagged = remote(asum0, asum0, 0, (1, py, px))
    pair2 = remote(own2, a2r, 8, (1, py, px))

    def second_ocean(c_one):
        ocean(b1, b2, True, True, True)
        send_edges(2, b2, 0, 2)
        if c_one:
            send_field(5, [(0, rise), (1, tfl)], f2s, f2r, True)
        else:
            send_field(5, [(0, rise), (1, tfl)], f2s, f2r)
            send_far()

    def first_tracer():
        tracer(f0r, None, 0, NS)
        light(own1)

        def visit(n, row, col, maybe):
            remote(own1.at[n], a1r.at[me], 7, (1, row, col)).start()

        half_peers(visit)

    ld_uv.wait()
    ld_t.wait()
    send_edges(0, b0)

    @pl.when(c == 0)
    def _():
        pltpu.make_async_copy(link, bands0, lsem.at[3]).wait()

        @pl.loop(0, 8)
        def _(i):
            sl = pl.ds(i * 4, 4)
            asum0[sl] = bands0[0, sl] + bands0[1, sl]

        lagged.start()

    @pl.when(c == 1)
    def _():
        for f in range(2):
            flux0[f].start()
        for f in range(2):
            ld_link(f).wait()

    step64 = lax.broadcasted_iota(jnp.int32, (NP, NP), 1).astype(F32)
    row64 = lax.broadcasted_iota(jnp.int32, (NP, NP), 0)
    held = jnp.where(owners[...] == me, 1.0, 0.0).astype(F32)
    placed = jnp.where(
        jnp.broadcast_to(owners[pl.ds(me, 1), :], (NP, NP)) == row64, 1.0, 0.0
    ).astype(F32)
    nt = (((1,), (1,)), ((), ()))
    steps8 = step64[0:8]
    for j, spots in enumerate((placed, held)):
        found = lax.dot_general(steps8, spots, nt, preferred_element_type=F32)
        inv_v[0:8, 64 * j : 64 * j + 64] = jnp.minimum(found, NP - 1.0).astype(jnp.int32)
    to_smem = pltpu.make_async_copy(inv_v, inv_s, lsem.at[6])
    to_smem.start()

    rows = lax.broadcasted_iota(jnp.int32, (K, K), 0)
    cols = lax.broadcasted_iota(jnp.int32, (K, K), 1)
    tabs[0] = jnp.where(rows < cols, 1.0, jnp.where(rows == cols, 0.5, 0.0)).astype(BF16)
    tabs[1] = jnp.where(rows >= cols, 1.0, 0.0).astype(BF16)
    tabs[2] = jnp.where(rows < cols, 1.0, 0.0).astype(BF16)
    r16 = lax.broadcasted_iota(jnp.int32, (128, 16), 0)
    c16 = lax.broadcasted_iota(jnp.int32, (128, 16), 1)
    spread = jnp.where(lax.shift_right_logical(r16, 3) == c16, 1.0, 0.0).astype(F32)
    r16t = lax.broadcasted_iota(jnp.int32, (16, 128), 0)
    c16t = lax.broadcasted_iota(jnp.int32, (16, 128), 1)
    spread_t = jnp.where(lax.shift_right_logical(c16t, 3) == r16t, 1.0, 0.0).astype(F32)
    wide = jnp.dot(
        jnp.dot(spread, mix[...], precision=lax.Precision.HIGHEST, preferred_element_type=F32),
        spread_t,
        precision=lax.Precision.HIGHEST,
        preferred_element_type=F32,
    )
    r128 = lax.broadcasted_iota(jnp.int32, (128, 128), 0)
    c128 = lax.broadcasted_iota(jnp.int32, (128, 128), 1)
    same = lax.bitwise_and(r128, 7) == lax.bitwise_and(c128, 7)
    wide = jnp.where(same, wide, 0.0)
    whi, wlo = split(wide)
    wmix[0:128, 0:128] = whi
    wmix[0:128, 128:256] = whi
    wmix[128:256, 0:128] = wlo
    wmix[128:256, 128:256] = jnp.zeros((128, 128), BF16)

    ones = jnp.ones((K, 128), BF16)
    depth[...] = (marine[...] * floor[...]).astype(F32)
    lev40 = lax.broadcasted_iota(jnp.int32, (40, 128), 1).astype(F32)
    spot = lax.broadcasted_iota(jnp.int32, (40, K), 0)
    spot = jnp.where(spot < 36, spot, spot - 40)
    column = lax.broadcasted_iota(jnp.int32, (40, K), 1)
    chosen = lax.bitwise_and(spot + (px * CX + K), K - 1) == column

    @pl.loop(0, 18)
    def _(y):
        gy = py * CY + y - 1
        inside = jnp.logical_and(gy >= 0, gy < 128)
        line = depth[pl.ds(jnp.clip(gy, 0, 127), 1), :]
        line = line * jnp.where(inside, 1.0, 0.0).astype(F32)
        d = dot(jnp.where(chosen, line, 0.0).astype(BF16), ones)
        w = jnp.concatenate(
            [
                jnp.where(lev40 < d, 1.0, 0.0).astype(F32),
                jnp.where(lev40 + 128.0 < d, 1.0, 0.0).astype(F32),
            ],
            axis=1,
        )
        wet_o[y] = w
        face_x[y] = w * pltpu.roll(w, 39, 0)

    @pl.loop(0, 17)
    def _(y):
        face_y[y] = wet_o[y, 0:32, :] * wet_o[y + 1, 0:32, :]

    to_smem.wait()
    ahead = lax.broadcasted_iota(jnp.int32, (8, K), 1) - lax.broadcasted_iota(
        jnp.int32, (8, K), 0
    )

    @pl.loop(0, 8)
    def _(i):
        for j in range(4):
            n = 4 * i + j
            s = spot_of(64 + 2 * n + par)
            line = depth[i * CY + lax.shift_right_logical(s, 2)]
            x0 = (2 * j + par) * CX + lax.bitwise_and(s, 3) * 8
            pick[n] = jnp.where(ahead == x0, jnp.broadcast_to(line[None, :], (8, K)), 0.0)

    depth_t[...] = dot(pick[...].reshape(NS * 8, K).astype(BF16), ones).reshape(NS, 8, 128)

    ld_c.wait()
    first_chl()
    light(None)
    take_edges(0, b0)
    ocean(b0, b1, True, True, True)

    @pl.when(c == 0)
    def _():
        first_heat()
        send_edges(1, b1)
        send_field(3, [(0, rise), (1, tfl)], f1s, f1r)
        for f in range(2):
            flux0[f].wait_recv()
        first_tracer()
        take_edges(1, b1)
        second_ocean(False)

    @pl.when(c == 1)
    def _():
        send_edges(1, b1, 0, 2)
        send_field(3, [(0, rise)], f1s, f1r)
        first_tracer()
        lagged.wait_recv()
        first_heat()
        send_edges(4, b1, 2, 3)
        send_field(4, [(1, tfl)], f1s, f1r)
        take_edges(1, b1, 0, 2)
        take_edges(4, b1, 2, 3)
        second_ocean(True)

    @pl.when(c == 0)
    def _():
        drain(f1r, xr_sem.at[3])

    @pl.when(c == 1)
    def _():
        drain(f1r.at[:, 0], xr_sem.at[3])
        drain(f1r.at[:, 1], xr_sem.at[4])

    tracer(f1r, None, 0, NS)
    light(own2)

    @pl.when(c == 0)
    def _():
        pair2.start()
        take_edges(2, b2, 0, 2)
        ocean(b2, None, False, False, True)
        send_all(9, 0, rise, True)

    @pl.when(c == 1)
    def _():
        drain(a1r, xr_sem.at[7])

        @pl.loop(0, 8)
        def _(i):
            for j in range(8):
                y = 2 * i + j // 4
                s = 8 * i + j
                b2[2, y + 1, pl.ds(8 * (j % 4), 8), :] = tfl[s] + 0.02 * a1r[own_s[me, s]]

        send_edges(3, b2, 2, 3)
        take_edges(2, b2, 0, 2)
        ocean(b2, None, False, False, True)
        send_all(9, 0, rise, False)

    drain(f2r, xr_sem.at[5])
    for j, (top, end) in enumerate(((0, 2), (2, 5), (5, 8))):
        tracer(f2r, own1, 4 * top, 4 * end)

        @pl.when(c == 0)
        def _(top=top, end=end):
            @pl.loop(4 * top, 4 * end)
            def _(n):
                start_or_keep(
                    chl_b.at[n], a3r.at[me], 11, 0, lax.div(n, 4), 2 * lax.rem(n, 4) + par
                )

        @pl.when(c == 1)
        def _(top=top, end=end):
            @pl.loop(0, end - top)
            def _(a):
                row = top + lax.rem(py + a, end - top)
                for bb in strip_cols:
                    remote(
                        chl_b.at[4 * row + bb], a3r.at[me], 11, (0, row, 2 * bb + par)
                    ).start()

        if j == 0:

            @pl.when(c == 1)
            def _():
                take_edges(3, b2, 2, 3)
                ocean(b2, None, False, True, False)
                send_all(10, 1, tfl, False)

    wait_edge_sends(0, b0)
    drain(own1, xs_sem.at[7])

    @pl.when(c == 0)
    def _():
        lagged.wait_send()
        pair2.wait_send()
        wait_edge_sends(1, b1)
        wait_edge_sends(2, b2, 0, 2)
        drain(f3s.at[0, 0:32], xs_sem.at[9])
        drain(f1s, xs_sem.at[3])
        drain(f2s, xs_sem.at[5])
        drain(a3r, xr_sem.at[11])

        @pl.loop(0, 8)
        def _(i):
            x = jnp.concatenate([a3r[own_s[me, i * 8 + j]] for j in range(8)], axis=0)
            i0, i1, h0, h1 = bands_of(x)
            wet = jnp.concatenate(
                [
                    wet_o[i * 2 + 1 + j // 4, pl.ds(8 * (j % 4), 8), :]
                    for j in range(8)
                ],
                axis=0,
            )
            sl = pl.ds(i * 8, 8)
            out[0, sl] = (wet * i0 * (1.0 - h0 * h0)).reshape(8, 8, K)
            out[1, sl] = (wet * i1 * (1.0 - h1 * h1)).reshape(8, 8, K)

    @pl.when(c == 1)
    def _():
        for f in range(2):
            flux0[f].wait_send()
        drain(f1s.at[:, 0], xs_sem.at[3])
        drain(f2s.at[0:16], xs_sem.at[5])
        drain(f1s.at[:, 1], xs_sem.at[4])
        wait_edge_sends(1, b1, 0, 2)
        wait_edge_sends(4, b1, 2, 3)
        wait_edge_sends(2, b2, 0, 2)
        wait_edge_sends(3, b2, 2, 3)
        drain(f3s.at[0, 0:32], xs_sem.at[9])
        drain(f3s.at[1], xs_sem.at[10])
        pair2.wait_recv()
        drain(f3r.at[0], xr_sem.at[9])
        drain(f3r.at[1], xr_sem.at[10])

        @pl.loop(0, NS)
        def _(n):
            mine = 2 * n + par
            other = 2 * n + (1 - par)
            out[0, mine] = f3r[0, mine]
            out[0, other] = f3r[0, other]
            out[1, mine] = f3r[1, mine] + 0.02 * own2[n]
            out[1, other] = f3r[1, other] + 0.02 * a2r[n]

    drain(chl_b, xs_sem.at[11])


def shards(
    current_speeds,
    thermal_anomaly,
    solute_amounts,
    delayed_link_source,
    marine_indicator,
    floor_layer_index,
    holder_rank,
    biota_exchange_matrix,
    photic_absorb_share,
    chroma_loading,
):
    any_spec = pl.BlockSpec(memory_space=pl.ANY)
    vmem = pl.BlockSpec(memory_space=pltpu.VMEM)
    smem = pl.BlockSpec(memory_space=pltpu.SMEM)

    def v(*shape, dtype=F32):
        return pltpu.VMEM(shape, dtype)

    dma = pltpu.SemaphoreType.DMA
    res = pl.pallas_call(
        kernel,
        out_shape=jax.ShapeDtypeStruct((2, NP, SC, K), F32),
        in_specs=[smem] * 3 + [any_spec] * 4 + [vmem] * 4,
        out_specs=vmem,
        scratch_shapes=[
            v(8, 128, dtype=jnp.int32),
            pltpu.SMEM((8, 128), jnp.int32),
            v(128, K),
            v(NS, SC, 128),
            v(NS, SC, K),
            v(18, 40, K),
            v(17, 32, K),
            v(5, 32, K),
            v(2, 128, K),
            v(2, 128, K),
            v(3, 18, 40, K),
            v(3, 18, 40, K),
            v(3, 18, 40, K),
            v(18, 40, K),
            v(18, 40, K),
            v(3, K, K, dtype=BF16),
            v(K, K, dtype=BF16),
            v(NTR, NS, SC, K),
            v(NS, SC, K),
            v(NS, SC, K),
            v(NP, SC, K),
            v(NP, SC, K),
            v(NP, SC, K),
            v(2, NS, 2, SC, K),
            v(NS, 2, SC, K),
            v(NS, 2, SC, K),
            v(NS, 2, SC, K),
            v(NS, 2, SC, K),
            v(48, 2, SC, K),
            v(NS, 2, SC, K),
            v(2, NP, SC, K),
            v(2, NP, SC, K),
            v(NS, SC, K),
            v(NS, SC, K),
            v(NP, SC, K),
            v(NS, SC, K),
            v(NP, SC, K),
            v(12, 2, SC, K),
            v(5, 2, 3, CY, K),
            v(5, 2, 3, CY, K),
            dma((7,)),
            dma((5, 4)),
            dma((5, 4)),
            dma((12,)),
            dma((12,)),
        ],
        compiler_params=pltpu.CompilerParams(
            collective_id=0, has_side_effects=True, vmem_limit_bytes=60 * 1024 * 1024
        ),
    )(
        holder_rank,
        photic_absorb_share,
        chroma_loading,
        current_speeds,
        thermal_anomaly,
        solute_amounts.reshape(NTR, NS, 2, SC, K),
        delayed_link_source.reshape(2, NS, 2, SC, K),
        marine_indicator,
        floor_layer_index,
        holder_rank,
        biota_exchange_matrix,
    )
    return res.reshape(1, 2, 1, 512, K)


def solution(mesh):
    placed = (
        P(None, "py", "px", None),
        P("py", "px", None),
        P(None, ("py", "px"), None, None),
        P("comp", None, ("py", "px"), None, None),
        P(),
        P(),
        P(),
        P(),
        P(),
        P(),
    )
    return jax.shard_map(
        shards,
        mesh=mesh,
        in_specs=placed,
        out_specs=P("comp", None, ("py", "px"), None, None),
        check_vma=False,
    )
```
